32 devices in a mesh: bf: 4 (over z), sk: 8 (over y, x, core).
Axes of the slice: x: 2, y: 2, z: 4, core: 2. Of those that a mesh axis runs over, the one named last changes fastest.
Arguments:
- kernel: bfloat16 [2, 8192, 16384], P(None, 'bf', 'sk'), may hold values from -1.5625 to 1.5625
- sketch: bfloat16 [3, 16384, 256], P(None, 'sk'), may hold values from -6 to 6
- projections: bfloat16 [2, 4, 2, 256, 128], P(None, 'bf'), may hold values from -0.375 to 0.375
- inverses: bfloat16 [2, 4, 2, 256, 256], P(None, 'bf'), may hold values from -0.375 to 0.375
- norm_gain: float32 [256], replicated, may hold values from 0.5 to 1.5
Outputs:
- factor_sketch: float32 [2, 3, 8192, 256], P(None, None, ('bf', 'sk'))
The draws below stay inside these ranges and needn't reach their ends.
All inputs are finite; a program needn't handle non-finite values.
Results may differ from the reference program's by a relative error of at most 0.02.
Values may be sent and summed in bfloat16 or wider, within the bound.
No kernel may reach another device: no remote copies, remote signals or barrier semaphores. Data moves between devices by JAX's collectives and lax.ppermute only.
A program may use at most 128 MiB of HBM per device.

```python
import math
import jax
import jax.numpy as jnp
from jax import lax

ROWS = 2048
SKETCH = 256
RANK = 128
PASSES = 3
LEVELS = 2
BLOCKS = 4
ROWS_ALL = 8192
COLS_ALL = 16384
N_BF = 4


def draw_kernel(key, part):
    key_rows = jax.random.fold_in(key, 11)
    key_cols = jax.random.fold_in(key, 12)
    key_vals = jax.random.fold_in(key, 13)
    col_scale = jnp.exp(jax.random.uniform(key_cols, (1, 1, COLS_ALL), jnp.float32, 0.0, math.log(10.0)))
    row_scale = jnp.exp(jax.random.uniform(key_rows, (1, ROWS_ALL, 1), jnp.float32, 0.0, math.log(10.0)))
    entries = jax.random.truncated_normal(key_vals, -6.0, 6.0, (2, ROWS_ALL, COLS_ALL), jnp.float32)
    values = entries * row_scale * col_scale / (3.0 * math.sqrt(COLS_ALL))
    return values.astype(jnp.bfloat16)


def level_of(stream_key, extent, cuts, low, largest):
    def one(position, blocks):
        draws = jax.random.uniform(jax.random.fold_in(jax.random.fold_in(stream_key, 6), position), (blocks,), jnp.float32, low / len(cuts), largest / len(cuts))
        return jnp.repeat(jnp.exp(draws), extent[position] // blocks).reshape((-1,) + (1,) * (len(extent) - position - 1))

    gain = one(*cuts[0])
    for cut in cuts[1:]:
        gain = gain * one(*cut)
    return gain


def gaussian(stream_key, shape, deviation, most, shards=(), kind=jnp.bfloat16):
    drawn = jax.random.normal(stream_key, shape, jnp.float32) * deviation
    if len(shards) > 0:
        drawn = level_of(stream_key, shape, shards, -0.22, 0.18) * drawn
    return jnp.clip(drawn, min=-most, max=most).astype(kind)


def setup_inputs(seed: int = 0) -> dict:
    keys = jax.random.split(jax.random.key(seed), 6)
    return {
        "kernel": draw_kernel(jax.random.fold_in(keys[5], 71), 0),
        "sketch": gaussian(keys[1], (PASSES, COLS_ALL, SKETCH), 1.0, 6.0, ((1, 8),)),
        "projections": gaussian(keys[2], (LEVELS, BLOCKS, 2, SKETCH, RANK), SKETCH ** -0.5, 0.375, ((1, 4),)),
        "inverses": gaussian(keys[3], (LEVELS, BLOCKS, 2, 2 * RANK, SKETCH), (2 * RANK) ** -0.5, 0.375, ((1, 4),)),
        "norm_gain": jnp.clip(1.0 + 0.1 * jax.random.normal(keys[4], (SKETCH,), jnp.float32), 0.5, 1.5),
    }


epsilon = 1e-06

def complex_level(real_in, imag_in, real_mat, imag_mat):
    real_in = real_in.astype(jnp.float32)
    imag_in = imag_in.astype(jnp.float32)
    real_mat = real_mat.astype(jnp.float32)
    imag_mat = imag_mat.astype(jnp.float32)
    real_out = jnp.einsum('pbrs,bsk->pbrk', real_in, real_mat) - jnp.einsum('pbrs,bsk->pbrk', imag_in, imag_mat)
    imag_out = jnp.einsum('pbrs,bsk->pbrk', real_in, imag_mat) + jnp.einsum('pbrs,bsk->pbrk', imag_in, real_mat)
    return (real_out, imag_out)

def reference(kernel, sketch, projections, inverses, norm_gain):
    real_blocks = []
    imag_blocks = []
    for block_idx in range(N_BF):
        kernel_re = kernel[0, block_idx * ROWS:(block_idx + 1) * ROWS]
        kernel_im = kernel[1, block_idx * ROWS:(block_idx + 1) * ROWS]
        proj_re = projections[0, block_idx, 0]
        proj_im = projections[0, block_idx, 1]
        real_pass = []
        imag_pass = []
        for pass_idx in range(PASSES):
            sk_re = jnp.dot(sketch[pass_idx], proj_re, preferred_element_type=jnp.float32).astype(jnp.bfloat16)
            sk_im = jnp.dot(sketch[pass_idx], proj_im, preferred_element_type=jnp.float32).astype(jnp.bfloat16)
            part_re = jnp.dot(kernel_re, sk_re, preferred_element_type=jnp.float32) - jnp.dot(kernel_im, sk_im, preferred_element_type=jnp.float32)
            part_im = jnp.dot(kernel_re, sk_im, preferred_element_type=jnp.float32) + jnp.dot(kernel_im, sk_re, preferred_element_type=jnp.float32)
            real_pass.append(part_re)
            imag_pass.append(part_im)
        real_blocks.append(jnp.stack(real_pass))
        imag_blocks.append(jnp.stack(imag_pass))
    own_re = jnp.stack(real_blocks, axis=1).astype(jnp.bfloat16)
    own_im = jnp.stack(imag_blocks, axis=1).astype(jnp.bfloat16)
    top_bits = N_BF.bit_length() - 1
    current_re = None
    current_im = None
    for level_idx in range(LEVELS):
        level_bit = top_bits - 1 - level_idx
        if level_idx > 0:
            rounded_re = current_re.astype(jnp.bfloat16)
            rounded_im = current_im.astype(jnp.bfloat16)
            own_re, own_im = complex_level(rounded_re, rounded_im, projections[level_idx, :, 0], projections[level_idx, :, 1])
            own_re = own_re.astype(jnp.bfloat16)
            own_im = own_im.astype(jnp.bfloat16)
        stride = 2 ** level_bit
        partner_re = jnp.flip(own_re.reshape(PASSES, N_BF // (2 * stride), 2, stride, ROWS, RANK), axis=2).reshape(PASSES, N_BF, ROWS, RANK)
        partner_im = jnp.flip(own_im.reshape(PASSES, N_BF // (2 * stride), 2, stride, ROWS, RANK), axis=2).reshape(PASSES, N_BF, ROWS, RANK)
        stacked_re = jnp.concatenate([own_re, partner_re], axis=-1)
        stacked_im = jnp.concatenate([own_im, partner_im], axis=-1)
        current_re, current_im = complex_level(stacked_re, stacked_im, inverses[level_idx, :, 0], inverses[level_idx, :, 1])
    power = lax.optimization_barrier(jnp.mean(current_re * current_re + current_im * current_im, axis=-1, keepdims=True))
    inv_rms = 1.0 / jnp.sqrt(power + epsilon)
    out_re = (current_re * inv_rms * norm_gain).reshape(PASSES, N_BF * ROWS, SKETCH)
    out_im = (current_im * inv_rms * norm_gain).reshape(PASSES, N_BF * ROWS, SKETCH)
    return jnp.stack([out_re, out_im])
```

```python
import functools
import jax
import jax.numpy as jnp
from jax import lax
from jax.experimental import pallas as pl
from jax.experimental.pallas import tpu as pltpu
from jax.sharding import PartitionSpec as P

epsilon = 1e-06
chunk_count = 4
depth_steps = 4
vmem_bytes = 56 * 1024 * 1024


def swapped(value, axis, mask):
    pairs = [(source, source ^ mask) for source in range(lax.axis_size(axis))]
    return lax.ppermute(value, axis, pairs)


def product(left, right):
    return lax.dot_general(left, right, (((1,), (0,)), ((), ())), preferred_element_type=jnp.float32)


def params():
    return pltpu.CompilerParams(vmem_limit_bytes=vmem_bytes)


def whole(shape):
    return pl.BlockSpec(shape, lambda *_: (0,) * len(shape))


def write_pieces(place_ref, acc_ref, keep_ref, send_ref, segments, chunk_rows, passes, rank):
    place = place_ref[0]
    for turn in range(segments):
        target = place ^ turn
        out_ref = send_ref if turn % 2 else keep_ref
        upper = acc_ref[pl.ds(pl.multiple_of(target * chunk_rows, chunk_rows), chunk_rows), :]
        lower = acc_ref[
            pl.ds(pl.multiple_of((segments + target) * chunk_rows, chunk_rows), chunk_rows), :
        ]
        for one in range(passes):
            re = slice(2 * one * rank, (2 * one + 1) * rank)
            im = slice((2 * one + 1) * rank, (2 * one + 2) * rank)
            out_ref[turn // 2, one, :, :rank] = (upper[:, re] - lower[:, im]).astype(jnp.bfloat16)
            out_ref[turn // 2, one, :, rank:] = (upper[:, im] + lower[:, re]).astype(jnp.bfloat16)


def gather_block(step, kernel_ref, value, acc_ref):
    block = kernel_ref[...].reshape(-1, kernel_ref.shape[3])
    part = product(block, value)

    @pl.when(step == 0)
    def _():
        acc_ref[...] = part

    @pl.when(step != 0)
    def _():
        acc_ref[...] += part


def first_body(place_ref, kernel_ref, sketch_ref, proj_ref, keep_ref, send_ref, sk_ref, acc_ref, *, sizes):
    segments, chunk_rows, passes, rank = sizes
    step = pl.program_id(0)
    both = jnp.concatenate([proj_ref[0, 0, 0], proj_ref[0, 0, 1]], axis=1)
    for one in range(passes):
        cols = slice(2 * one * rank, 2 * (one + 1) * rank)
        sk_ref[:, cols] = product(sketch_ref[one], both).astype(jnp.bfloat16)
    gather_block(step, kernel_ref, sk_ref[...], acc_ref)

    @pl.when(step == pl.num_programs(0) - 1)
    def _():
        write_pieces(place_ref, acc_ref, keep_ref, send_ref, segments, chunk_rows, passes, rank)


def later_body(place_ref, kernel_ref, sk_ref, keep_ref, send_ref, acc_ref, *, sizes):
    segments, chunk_rows, passes, rank = sizes
    step = pl.program_id(0)
    gather_block(step, kernel_ref, sk_ref[...], acc_ref)

    @pl.when(step == pl.num_programs(0) - 1)
    def _():
        write_pieces(place_ref, acc_ref, keep_ref, send_ref, segments, chunk_rows, passes, rank)


def gathered(place, kernel, chunk, chunk_rows, sketch, first_proj, sk_value):
    _, segments, _, cols = kernel.shape
    passes, _, sketch_cols = sketch.shape
    rank = first_proj.shape[4]
    width = 2 * passes * rank
    deep = cols // depth_steps
    sizes = (segments, chunk_rows, passes, rank)
    piece = jax.ShapeDtypeStruct((segments // 2, passes, chunk_rows, 2 * rank), jnp.bfloat16)
    place_spec = pl.BlockSpec(memory_space=pltpu.SMEM)
    kernel_spec = pl.BlockSpec((2, segments, chunk_rows, deep), lambda k: (0, 0, chunk, k))
    scratch = [pltpu.VMEM((2 * segments * chunk_rows, width), jnp.float32)]
    cost = pl.CostEstimate(
        flops=4 * segments * chunk_rows * cols * width,
        bytes_accessed=4 * segments * chunk_rows * cols + 2 * cols * width,
        transcendentals=0,
    )
    if sk_value is None:
        return pl.pallas_call(
            functools.partial(first_body, sizes=sizes),
            name="gather_first",
            grid=(depth_steps,),
            in_specs=[
                place_spec,
                kernel_spec,
                pl.BlockSpec((passes, deep, sketch_cols), lambda k: (0, k, 0)),
                pl.BlockSpec((1, 1, 2, sketch_cols, rank), lambda k: (0, 0, 0, 0, 0)),
            ],
            out_specs=[whole(piece.shape), whole(piece.shape), pl.BlockSpec((deep, width), lambda k: (k, 0))],
            out_shape=[piece, piece, jax.ShapeDtypeStruct((cols, width), jnp.bfloat16)],
            scratch_shapes=scratch,
            compiler_params=params(),
            cost_estimate=cost,
        )(place, kernel, sketch, first_proj)
    return pl.pallas_call(
        functools.partial(later_body, sizes=sizes),
        name="gather_later",
        grid=(depth_steps,),
        in_specs=[place_spec, kernel_spec, pl.BlockSpec((deep, width), lambda k: (k, 0))],
        out_specs=[whole(piece.shape), whole(piece.shape)],
        out_shape=[piece, piece],
        scratch_shapes=scratch,
        compiler_params=params(),
        cost_estimate=cost,
    )(place, kernel, sk_value)


def weights_body(proj_ref, inv_ref, *out_refs):
    levels = proj_ref.shape[0]
    rank = proj_ref.shape[4]
    for level in range(levels):
        for half in range(2):
            rows = slice(half * rank, (half + 1) * rank)
            re = inv_ref[level, 0, 0, rows, :]
            im = inv_ref[level, 0, 1, rows, :]
            if level + 1 < levels:
                next_re = proj_ref[level + 1, 0, 0]
                next_im = proj_ref[level + 1, 0, 1]
                re, im = (
                    (product(re, next_re) - product(im, next_im)).astype(jnp.bfloat16),
                    (product(re, next_im) + product(im, next_re)).astype(jnp.bfloat16),
                )
            cols = re.shape[1]
            out_refs[level][half * 2 * rank : half * 2 * rank + rank, :cols] = re
            out_refs[level][half * 2 * rank : half * 2 * rank + rank, cols:] = im
            out_refs[level][half * 2 * rank + rank : (half + 1) * 2 * rank, :cols] = -im
            out_refs[level][half * 2 * rank + rank : (half + 1) * 2 * rank, cols:] = re


def level_weights(projections, inverses):
    levels = projections.shape[0]
    rank = projections.shape[4]
    sketch_cols = inverses.shape[4]
    shapes = [
        jax.ShapeDtypeStruct((4 * rank, 2 * (rank if level + 1 < levels else sketch_cols)), jnp.bfloat16)
        for level in range(levels)
    ]
    return pl.pallas_call(
        weights_body, name="level_weights", out_shape=shapes, compiler_params=params()
    )(projections, inverses)


def paired(own_ref, partner_ref, weight_ref):
    width = own_ref.shape[2]
    own = own_ref[...].reshape(-1, width)
    partner = partner_ref[...].reshape(-1, width)
    return product(own, weight_ref[:width, :]) + product(partner, weight_ref[width:, :])


def middle_body(own_ref, partner_ref, weight_ref, out_ref):
    out_ref[...] = paired(own_ref, partner_ref, weight_ref).astype(jnp.bfloat16).reshape(out_ref.shape)


def middle_level(own, partner, weight):
    return pl.pallas_call(
        middle_body,
        name="middle_level",
        out_shape=jax.ShapeDtypeStruct(own.shape, jnp.bfloat16),
        compiler_params=params(),
    )(own, partner, weight)


def final_body(own_ref, partner_ref, weight_ref, gain_ref, *rest):
    out_ref = rest[-1]
    current = paired(own_ref, partner_ref, weight_ref)
    sketch_cols = gain_ref.shape[1]
    power = jnp.sum(current * current, axis=-1, keepdims=True) / sketch_cols
    scale = lax.rsqrt(power + epsilon)
    shape = out_ref.shape[1:]
    gain = gain_ref[...]
    out_ref[0] = (current[:, :sketch_cols] * scale * gain).reshape(shape)
    out_ref[1] = (current[:, sketch_cols:] * scale * gain).reshape(shape)


def final_level(own, partner, weight, gain, out, chunk, segment_rows):
    passes, chunk_rows, _ = own.shape
    sketch_cols = gain.shape[1]
    operands = [own, partner, weight, gain]
    specs = [whole(value.shape) for value in operands]
    aliases = {}
    if out is not None:
        operands.append(out)
        specs.append(pl.BlockSpec(memory_space=pl.ANY))
        aliases = {4: 0}
    return pl.pallas_call(
        final_body,
        name="final_level",
        grid=(1,),
        in_specs=specs,
        out_specs=pl.BlockSpec((2, passes, chunk_rows, sketch_cols), lambda i: (0, 0, chunk, 0)),
        out_shape=jax.ShapeDtypeStruct((2, passes, segment_rows, sketch_cols), jnp.float32),
        input_output_aliases=aliases,
        compiler_params=params(),
    )(*operands)


def shards(kernel, sketch, projections, inverses, norm_gain):
    members = lax.axis_size("sk")
    levels = projections.shape[0]
    top_bits = lax.axis_size("bf").bit_length() - 1
    _, rows, cols = kernel.shape
    segment_rows = rows // members
    chunk_rows = segment_rows // chunk_count
    kernel = kernel.reshape(2, members, segment_rows, cols)
    place = lax.axis_index("sk").reshape(1).astype(jnp.int32)
    gain = norm_gain.reshape(1, -1)
    weights = level_weights(projections, inverses)
    out = None
    sk_value = None
    for chunk in range(chunk_count):
        results = gathered(place, kernel, chunk, chunk_rows, sketch, projections, sk_value)
        keep, send = results[:2]
        if sk_value is None:
            sk_value = results[2]
        both = keep.astype(jnp.float32) + swapped(send, "sk", 1).astype(jnp.float32)
        own = both[0]
        for turn in range(1, members // 2):
            own = own + swapped(both[turn].astype(jnp.bfloat16), "sk", 2 * turn).astype(jnp.float32)
        own = own.astype(jnp.bfloat16)
        for level in range(levels):
            partner = swapped(own, "bf", 2 ** (top_bits - 1 - level))
            if level + 1 < levels:
                own = middle_level(own, partner, weights[level])
            else:
                out = final_level(own, partner, weights[level], gain, out, chunk, segment_rows)
    return out


def solution(mesh):
    placed = (
        P(None, "bf", "sk"),
        P(None, "sk", None),
        P(None, "bf", None, None, None),
        P(None, "bf", None, None, None),
        P(),
    )
    return jax.shard_map(
        shards,
        mesh=mesh,
        in_specs=placed,
        out_specs=P(None, None, ("bf", "sk"), None),
        check_vma=False,
    )
```

```python
import functools
import jax
import jax.numpy as jnp
from jax import lax
from jax.experimental import pallas as pl
from jax.experimental.pallas import tpu as pltpu
from jax.sharding import PartitionSpec as P

epsilon = 1e-06
shares = (3, 2, 2, 1)
groups = ((0,), (1,), (2,), (3,))
exchanges = (((0, 0),), ((0, 1),), ((1, 0),), ((1, 1),), ((2, 0),), ((2, 1),), ((3, 0),), ((3, 1),))
project_steps = 4
mib = 1024 * 1024
in_vmem = pl.BlockSpec(memory_space=pltpu.VMEM)
in_hbm = pl.BlockSpec(memory_space=pltpu.HBM)
in_smem = pl.BlockSpec(memory_space=pltpu.SMEM)


def swapped(value, axis, mask):
    pairs = [(source, source ^ mask) for source in range(lax.axis_size(axis))]
    return lax.ppermute(value, axis, pairs)


def phase_count(members):
    return members.bit_length() - 2


def chip_bit(core, step, count):
    return (core + step) % count


def swapped_step(value, step):
    members = lax.axis_size("sk")
    count = phase_count(members)
    pairs = [
        (source, source ^ (2 << chip_bit(source % 2, step, count))) for source in range(members)
    ]
    return lax.ppermute(value, "sk", pairs)


def product(left, right):
    return lax.dot_general(left, right, (((1,), (0,)), ((), ())), preferred_element_type=jnp.float32)


def params(megabytes):
    return pltpu.CompilerParams(vmem_limit_bytes=megabytes * mib)


def local(value):
    return pltpu.with_memory_space_constraint(value, pltpu.VMEM)


def remote(value):
    return pltpu.with_memory_space_constraint(value, pltpu.HBM)


def piece_target(place, index, segments, chunk):
    count = phase_count(segments)
    turns = []
    for core in range(2):
        turn = 0
        for phase in range(count):
            if (index >> (count - 1 - phase)) & 1:
                turn |= 2 << chip_bit(core, chunk + phase, count)
        turns.append(turn)
    return place ^ jnp.where(place % 2 == 0, turns[0], turns[1])


def write_pieces(place, acc_ref, keep_ref, send_ref, chunk):
    halves, passes, chunk_rows, width = keep_ref.shape
    rank = width // 2
    segments = 2 * halves
    for turn in range(segments):
        out_ref = send_ref if turn % 2 else keep_ref
        target = piece_target(place ^ (turn % 2), turn // 2, segments, chunk)
        rows = pl.ds(pl.multiple_of(target * chunk_rows, chunk_rows), chunk_rows)
        upper = acc_ref[0, rows, :]
        lower = acc_ref[1, rows, :]
        for one in range(passes):
            re = slice(2 * one * rank, (2 * one + 1) * rank)
            im = slice((2 * one + 1) * rank, (2 * one + 2) * rank)
            out_ref[turn // 2, one, :, :rank] = (upper[:, re] - lower[:, im]).astype(jnp.bfloat16)
            out_ref[turn // 2, one, :, rank:] = (upper[:, im] + lower[:, re]).astype(jnp.bfloat16)


def block_copies(kernel_ref, block_ref, sems, span, part):
    return [
        pltpu.make_async_copy(
            kernel_ref.at[part, segment, pl.ds(*span), :],
            block_ref.at[part, segment],
            sems.at[part, segment],
        )
        for segment in range(block_ref.shape[1])
    ]


def both_copies(kernel_ref, block_ref, sems, span):
    return [copy for part in range(2) for copy in block_copies(kernel_ref, block_ref, sems, span, part)]


def first_body(place_ref, kernel_ref, sketch_ref, proj_ref, *rest, spans):
    if len(spans) > 1:
        keep_ref, send_ref, sk_ref, next_ref, *rest = rest
        *rest, next_sems = rest
    else:
        keep_ref, send_ref, sk_ref, *rest = rest
    held_ref, parts_ref, block_ref, acc_ref, sketch_sems, proj_sem, block_sems = rest
    passes, cols, _ = sketch_ref.shape
    rank = proj_ref.shape[4]
    deep = cols // project_steps

    def sketch_copy(step):
        rows = pl.ds(pl.multiple_of(step * deep, deep), deep)
        return pltpu.make_async_copy(
            sketch_ref.at[:, rows, :], held_ref.at[:, rows, :], sketch_sems.at[step]
        )

    proj_copy = pltpu.make_async_copy(proj_ref.at[0, 0], parts_ref, proj_sem)
    proj_copy.start()
    for step in range(project_steps):
        sketch_copy(step).start()
    for copy in block_copies(kernel_ref, block_ref, block_sems, spans[0], 0):
        copy.start()
    next_copies = []
    if len(spans) > 1:
        next_copies = both_copies(kernel_ref, next_ref, next_sems, spans[1])
    proj_copy.wait()

    def project(step, carry):
        sketch_copy(step).wait()
        both = jnp.concatenate([parts_ref[0], parts_ref[1]], axis=1)
        rows = pl.ds(pl.multiple_of(step * deep, deep), deep)
        for one in range(passes):
            cols = slice(2 * one * rank, 2 * (one + 1) * rank)
            sk_ref[rows, cols] = product(held_ref[one, rows, :], both).astype(jnp.bfloat16)
        return carry

    def gather(part, carry):
        for copy in block_copies(kernel_ref, block_ref, block_sems, spans[0], part):
            copy.wait()

        @pl.when(part == 0)
        def _():
            for copy in next_copies:
                copy.start()

        acc_ref[part] = product(block_ref[part].reshape(-1, cols), sk_ref[...])
        return carry

    lax.fori_loop(0, 1, project, 0)
    for copy in block_copies(kernel_ref, block_ref, block_sems, spans[0], 1):
        copy.start()
    lax.fori_loop(1, project_steps, project, 0)
    lax.fori_loop(0, 2, gather, 0)
    write_pieces(place_ref[0], acc_ref, keep_ref, send_ref, 0)
    for copy in next_copies:
        copy.wait()


def cost_of(kernel, span, width):
    _, segments, _, cols = kernel.shape
    return pl.CostEstimate(
        flops=4 * segments * span[1] * cols * width,
        bytes_accessed=4 * segments * span[1] * cols,
        transcendentals=0,
    )


def first_gathered(place, kernel, sketch, projections, spans):
    _, segments, _, cols = kernel.shape
    passes, _, sketch_cols = sketch.shape
    rank = projections.shape[4]
    width = 2 * passes * rank
    piece = pltpu.VMEM((segments // 2, passes, spans[0][1], 2 * rank), jnp.bfloat16)
    out_shape = [piece, piece, pltpu.VMEM((cols, width), jnp.bfloat16)]
    scratch = [
        pltpu.VMEM(sketch.shape, sketch.dtype),
        pltpu.VMEM((2, sketch_cols, rank), projections.dtype),
        pltpu.VMEM((2, segments, spans[0][1], cols), kernel.dtype),
        pltpu.VMEM((2, segments * spans[0][1], width), jnp.float32),
        pltpu.SemaphoreType.DMA((project_steps,)),
        pltpu.SemaphoreType.DMA(()),
        pltpu.SemaphoreType.DMA((2, segments)),
    ]
    if len(spans) > 1:
        out_shape.append(pltpu.VMEM((2, segments, spans[1][1], cols), kernel.dtype))
        scratch.append(pltpu.SemaphoreType.DMA((2, segments)))
    return pl.pallas_call(
        functools.partial(first_body, spans=spans),
        name="gather_first",
        in_specs=[in_smem, in_hbm, in_hbm, in_hbm],
        out_specs=[in_vmem] * len(out_shape),
        out_shape=out_shape,
        scratch_shapes=scratch,
        compiler_params=params(28),
        cost_estimate=cost_of(kernel, spans[0], width),
    )(place, remote(kernel), remote(sketch), remote(projections))


def gather_body(place_ref, block_ref, sk_ref, *rest, chunk, next_span):
    step = pl.program_id(0)
    copies = []
    if next_span is None:
        keep_ref, send_ref, acc_ref = rest
    else:
        kernel_ref, keep_ref, send_ref, next_ref, acc_ref, sems = rest
        copies = both_copies(kernel_ref, next_ref, sems, next_span)

        @pl.when(step == 0)
        def _():
            for copy in copies:
                copy.start()

    cols = block_ref.shape[3]
    acc_ref[step] = product(block_ref[step].reshape(-1, cols), sk_ref[...])

    @pl.when(step == 1)
    def _():
        write_pieces(place_ref[0], acc_ref, keep_ref, send_ref, chunk)
        for copy in copies:
            copy.wait()


def gathered(place, block, sk_value, kernel, passes, chunk, spans):
    _, segments, chunk_rows, cols = block.shape
    width = sk_value.shape[1]
    piece = pltpu.VMEM((segments // 2, passes, chunk_rows, width // passes), jnp.bfloat16)
    operands = [place, local(block), local(sk_value)]
    in_specs = [in_smem, in_vmem, in_vmem]
    out_shape = [piece, piece]
    scratch = [pltpu.VMEM((2, segments * chunk_rows, width), jnp.float32)]
    next_span = spans[chunk + 1] if chunk + 1 < len(spans) else None
    if next_span is not None:
        operands.append(remote(kernel))
        in_specs.append(in_hbm)
        out_shape.append(pltpu.VMEM((2, segments, next_span[1], cols), jnp.bfloat16))
        scratch.append(pltpu.SemaphoreType.DMA((2, segments)))
    return pl.pallas_call(
        functools.partial(gather_body, chunk=chunk, next_span=next_span),
        name="gather",
        grid=(2,),
        in_specs=in_specs,
        out_specs=[in_vmem] * len(out_shape),
        out_shape=out_shape,
        scratch_shapes=scratch,
        compiler_params=params(12),
        cost_estimate=cost_of(kernel, spans[chunk], width),
    )(*operands)


def sum_body(*refs, stages):
    for held, got, got_row, hold, send, send_row, own in stages:
        total = refs[held][...].astype(jnp.float32)
        width = total.shape[3]
        if got_row is None:
            total = total + refs[got][...].astype(jnp.float32)
        else:
            rows = total.size // width
            total = total + refs[got][got_row : got_row + rows, :].astype(jnp.float32).reshape(total.shape)
        half = total.shape[0] // 2
        if own is None:
            flat = total[half:].astype(jnp.bfloat16).reshape(-1, width)
            refs[hold][...] = total[:half]
            refs[send][send_row : send_row + flat.shape[0], :] = flat
        else:
            refs[own][...] = total[0].astype(jnp.bfloat16)


def summed(parts, count):
    operands = []
    out_shape = []
    entries = []
    send_row = 0
    for phase, held, got, got_row in parts:
        pieces = 1 << (count - phase)
        passes, chunk_rows, width = held.shape[1:]
        entry = [len(operands), len(operands) + 1, got_row, None, None, None, None]
        operands.extend([local(held), local(got)])
        if phase == count:
            entry[6] = len(out_shape)
            out_shape.append(pltpu.VMEM((passes, chunk_rows, width), jnp.bfloat16))
        else:
            entry[3] = len(out_shape)
            entry[5] = send_row
            send_row += passes * chunk_rows * (pieces // 2)
            out_shape.append(pltpu.VMEM((pieces // 2, passes, chunk_rows, width), jnp.float32))
        entries.append(entry)
    if send_row:
        out_shape.append(pltpu.VMEM((send_row, width), jnp.bfloat16))
    for entry in entries:
        if entry[6] is None:
            entry[3] += len(operands)
            entry[4] = len(operands) + len(out_shape) - 1
        else:
            entry[6] += len(operands)
    results = pl.pallas_call(
        functools.partial(sum_body, stages=tuple(map(tuple, entries))),
        name="sum_parts",
        in_specs=[in_vmem] * len(operands),
        out_specs=[in_vmem] * len(out_shape),
        out_shape=out_shape,
        compiler_params=params(8),
    )(*operands)
    return results


def plan_of(count):
    if count == 2:
        return exchanges
    chunks = len(shares)
    return tuple(
        tuple((step - phase, phase) for phase in range(count) if 0 <= step - phase < chunks)
        for step in range(chunks + count - 1)
    )


def weights_body(proj_ref, inv_ref, *out_refs):
    levels = proj_ref.shape[0]
    rank = proj_ref.shape[4]
    for level in range(levels):
        for half in range(2):
            rows = slice(half * rank, (half + 1) * rank)
            re = inv_ref[level, 0, 0, rows, :]
            im = inv_ref[level, 0, 1, rows, :]
            if level + 1 < levels:
                next_re = proj_ref[level + 1, 0, 0]
                next_im = proj_ref[level + 1, 0, 1]
                re, im = (
                    (product(re, next_re) - product(im, next_im)).astype(jnp.bfloat16),
                    (product(re, next_im) + product(im, next_re)).astype(jnp.bfloat16),
                )
            cols = re.shape[1]
            out_refs[level][half * 2 * rank : half * 2 * rank + rank, :cols] = re
            out_refs[level][half * 2 * rank : half * 2 * rank + rank, cols:] = im
            out_refs[level][half * 2 * rank + rank : (half + 1) * 2 * rank, :cols] = -im
            out_refs[level][half * 2 * rank + rank : (half + 1) * 2 * rank, cols:] = re


def level_weights(projections, inverses):
    levels = projections.shape[0]
    rank = projections.shape[4]
    sketch_cols = inverses.shape[4]
    shapes = [
        pltpu.VMEM((4 * rank, 2 * (rank if level + 1 < levels else sketch_cols)), jnp.bfloat16)
        for level in range(levels)
    ]
    return pl.pallas_call(
        weights_body,
        name="level_weights",
        out_specs=[in_vmem] * levels,
        out_shape=shapes,
        compiler_params=params(8),
    )(projections, inverses)


def paired(own, partner, weight_ref):
    width = own.shape[-1]
    own = own.reshape(-1, width)
    partner = partner.reshape(-1, width)
    return product(own, weight_ref[:width, :]) + product(partner, weight_ref[width:, :])


def middle_body(*refs, count):
    weight_ref = refs[2 * count]
    out_ref = refs[2 * count + 1]
    first = 0
    for place in range(count):
        own = refs[place][...]
        rows = own.shape[1]
        value = paired(own, refs[count + place][...], weight_ref)
        out_ref[:, first : first + rows, :] = value.astype(jnp.bfloat16).reshape(own.shape)
        first += rows


def middle_level(owns, partners, weight):
    passes, _, width = owns[0].shape
    rows = sum(own.shape[1] for own in owns)
    operands = [local(value) for value in (*owns, *partners, weight)]
    return pl.pallas_call(
        functools.partial(middle_body, count=len(owns)),
        name="middle_level",
        in_specs=[in_vmem] * len(operands),
        out_specs=in_vmem,
        out_shape=pltpu.VMEM((passes, rows, width), jnp.bfloat16),
        compiler_params=params(4),
    )(*operands)


def normalized(own_ref, partner_ref, weight_ref, gain_ref):
    current = paired(own_ref[...], partner_ref[...], weight_ref)
    sketch_cols = gain_ref.shape[1]
    power = jnp.sum(current * current, axis=-1, keepdims=True) / sketch_cols
    scale = lax.rsqrt(power + epsilon)
    gain = gain_ref[...]
    shape = own_ref.shape[:2] + (sketch_cols,)
    return (
        (current[:, :sketch_cols] * scale * gain).reshape(shape),
        (current[:, sketch_cols:] * scale * gain).reshape(shape),
    )


def staged_body(own_ref, partner_ref, weight_ref, gain_ref, stage_ref):
    stage_ref[0], stage_ref[1] = normalized(own_ref, partner_ref, weight_ref, gain_ref)


def staged_level(own, partner, weight, gain):
    passes, rows, _ = own.shape
    return pl.pallas_call(
        staged_body,
        name="staged_level",
        in_specs=[in_vmem] * 4,
        out_specs=in_vmem,
        out_shape=pltpu.VMEM((2, passes, rows, gain.shape[1]), jnp.float32),
        compiler_params=params(8),
    )(local(own), local(partner), local(weight), local(gain))


def final_body(own_ref, partner_ref, weight_ref, gain_ref, *rest, firsts):
    stages = rest[: len(firsts) - 1]
    out_ref, stage_ref, sems = rest[len(firsts) - 1 :]
    copies = []
    for place, (first, part_ref) in enumerate(zip(firsts, (*stages, stage_ref))):
        target = out_ref.at[:, :, pl.ds(first, part_ref.shape[2]), :]
        copies.append(pltpu.make_async_copy(part_ref, target, sems.at[place]))
    for copy in copies[:-1]:
        copy.start()
    stage_ref[0], stage_ref[1] = normalized(own_ref, partner_ref, weight_ref, gain_ref)
    copies[-1].start()
    for copy in copies:
        copy.wait()


def final_level(own, partner, weight, gain, stages, firsts, segment_rows):
    passes, rows, _ = own.shape
    sketch_cols = gain.shape[1]
    operands = [local(value) for value in (own, partner, weight, gain, *stages)]
    return pl.pallas_call(
        functools.partial(final_body, firsts=tuple(firsts)),
        name="final_level",
        in_specs=[in_vmem] * len(operands),
        out_specs=in_hbm,
        out_shape=jax.ShapeDtypeStruct((2, passes, segment_rows, sketch_cols), jnp.float32),
        scratch_shapes=[
            pltpu.VMEM((2, passes, rows, sketch_cols), jnp.float32),
            pltpu.SemaphoreType.DMA((len(firsts),)),
        ],
        compiler_params=params(8),
    )(*operands)


def shards(kernel, sketch, projections, inverses, norm_gain):
    members = lax.axis_size("sk")
    count = phase_count(members)
    levels = projections.shape[0]
    passes = sketch.shape[0]
    top_bits = lax.axis_size("bf").bit_length() - 1
    _, rows, cols = kernel.shape
    segment_rows = rows // members
    unit = segment_rows // sum(shares)
    spans = []
    for share in shares:
        first = spans[-1][0] + spans[-1][1] if spans else 0
        spans.append((first, share * unit))
    chunks = len(spans)
    kernel = kernel.reshape(2, members, segment_rows, cols)
    place = lax.axis_index("sk").reshape(1).astype(jnp.int32)
    gain = norm_gain.reshape(1, -1)
    weights = level_weights(projections, inverses)
    keeps = []
    cores = []
    block = None
    for chunk in range(chunks):
        if chunk == 0:
            keep, send, sk_value, *blocks = first_gathered(place, kernel, sketch, projections, spans)
        else:
            keep, send, *blocks = gathered(place, block, sk_value, kernel, passes, chunk, spans)
        if blocks:
            block = blocks[0]
        keeps.append(keep)
        cores.append(swapped(send, "sk", 1))
    held = dict(enumerate(keeps))
    got = {chunk: (core, None) for chunk, core in enumerate(cores)}
    for place, exchange in enumerate(plan_of(count)):
        parts = [(phase, held[chunk], *got[chunk]) for chunk, phase in exchange]
        *kept, send = summed(parts, count)
        chunk, phase = exchange[0]
        received = swapped_step(send, chunk + phase)
        row = 0
        for (chunk, _), value in zip(exchange, kept):
            held[chunk] = value
            got[chunk] = (received, row)
            row += value.size // value.shape[3]
    owns = []
    for chunk in range(chunks):
        owns.extend(summed([(count, held[chunk], *got[chunk])], count))
    partners = []
    for chunk in range(chunks):
        partners.append(swapped(owns[chunk], "bf", 2 ** (top_bits - 1)))
    stages = []
    firsts = []
    for place, group in enumerate(groups):
        own = [owns[chunk] for chunk in group]
        partner = [partners[chunk] for chunk in group]
        for level in range(1, levels):
            merged = middle_level(own, partner, weights[level - 1])
            own = [merged]
            partner = [swapped(merged, "bf", 2 ** (top_bits - 1 - level))]
        firsts.append(spans[group[0]][0])
        if place + 1 < len(groups):
            stages.append(staged_level(own[0], partner[0], weights[levels - 1], gain))
        else:
            out = final_level(
                own[0], partner[0], weights[levels - 1], gain, stages, firsts, segment_rows
            )
    return out


def solution(mesh):
    placed = (
        P(None, "bf", "sk"),
        P(None, "sk", None),
        P(None, "bf", None, None, None),
        P(None, "bf", None, None, None),
        P(),
    )

    return jax.shard_map(
        shards,
        mesh=mesh,
        in_specs=placed,
        out_specs=P(None, None, ("bf", "sk"), None),
        check_vma=False,
    )
```

```python
import functools
import jax
import jax.numpy as jnp
from jax import lax
from jax.experimental import pallas as pl
from jax.experimental.pallas import tpu as pltpu
from jax.sharding import PartitionSpec as P

epsilon = 1e-06
shares = (2, 2, 2, 2)
splits = (1, 1, 1, 1)
groups = ((0,), (1,), (2,), (3,))
exchanges = (((0, 0),), ((0, 1), (1, 0)), ((1, 1),), ((2, 0),), ((2, 1),), ((3, 0),), ((3, 1),))
project_steps = 4
mib = 1024 * 1024
in_vmem = pl.BlockSpec(memory_space=pltpu.VMEM)
in_hbm = pl.BlockSpec(memory_space=pltpu.HBM)
in_smem = pl.BlockSpec(memory_space=pltpu.SMEM)


def swapped(value, axis, mask):
    pairs = [(source, source ^ mask) for source in range(lax.axis_size(axis))]
    return lax.ppermute(value, axis, pairs)


def phase_count(members):
    return members.bit_length() - 2


def chip_bit(core, step, count):
    return (core + step) % count


def swapped_step(value, step):
    members = lax.axis_size("sk")
    count = phase_count(members)
    pairs = [
        (source, source ^ (2 << chip_bit(source % 2, step, count))) for source in range(members)
    ]
    return lax.ppermute(value, "sk", pairs)


def product(left, right):
    return lax.dot_general(left, right, (((1,), (0,)), ((), ())), preferred_element_type=jnp.float32)


def params(megabytes):
    return pltpu.CompilerParams(vmem_limit_bytes=megabytes * mib)


def local(value):
    return pltpu.with_memory_space_constraint(value, pltpu.VMEM)


def remote(value):
    return pltpu.with_memory_space_constraint(value, pltpu.HBM)


def piece_target(place, index, segments, chunk):
    count = phase_count(segments)
    turns = []
    for core in range(2):
        turn = 0
        for phase in range(count):
            if (index >> (count - 1 - phase)) & 1:
                turn |= 2 << chip_bit(core, chunk + phase, count)
        turns.append(turn)
    return place ^ jnp.where(place % 2 == 0, turns[0], turns[1])


def write_pieces(place, acc_ref, keep_ref, send_ref, chunk, first, chunk_rows):
    halves, passes, _, width = keep_ref.shape
    kept = slice(first, first + chunk_rows)
    rank = width // 2
    segments = 2 * halves
    for turn in range(segments):
        out_ref = send_ref if turn % 2 else keep_ref
        target = piece_target(place ^ (turn % 2), turn // 2, segments, chunk)
        rows = pl.ds(pl.multiple_of(target * chunk_rows, chunk_rows), chunk_rows)
        upper = acc_ref[0, rows, :]
        lower = acc_ref[1, rows, :]
        for one in range(passes):
            re = slice(2 * one * rank, (2 * one + 1) * rank)
            im = slice((2 * one + 1) * rank, (2 * one + 2) * rank)
            out_ref[turn // 2, one, kept, :rank] = (upper[:, re] - lower[:, im]).astype(jnp.bfloat16)
            out_ref[turn // 2, one, kept, rank:] = (upper[:, im] + lower[:, re]).astype(jnp.bfloat16)


def block_copies(kernel_ref, block_ref, sems, span, part):
    return [
        pltpu.make_async_copy(
            kernel_ref.at[part, segment, pl.ds(*span), :],
            block_ref.at[part, segment],
            sems.at[part, segment],
        )
        for segment in range(block_ref.shape[1])
    ]


def both_copies(kernel_ref, block_ref, sems, span):
    return [copy for part in range(2) for copy in block_copies(kernel_ref, block_ref, sems, span, part)]


def first_body(place_ref, kernel_ref, sketch_ref, proj_ref, *rest, spans):
    if len(spans) > 1:
        keep_ref, send_ref, sk_ref, next_ref, *rest = rest
        *rest, next_sems = rest
    else:
        keep_ref, send_ref, sk_ref, *rest = rest
    held_ref, parts_ref, block_ref, acc_ref, sketch_sems, proj_sem, block_sems = rest
    passes, cols, _ = sketch_ref.shape
    rank = proj_ref.shape[4]
    deep = cols // project_steps

    def sketch_copy(step):
        rows = pl.ds(pl.multiple_of(step * deep, deep), deep)
        return pltpu.make_async_copy(
            sketch_ref.at[:, rows, :], held_ref.at[:, rows, :], sketch_sems.at[step]
        )

    proj_copy = pltpu.make_async_copy(proj_ref.at[0, 0], parts_ref, proj_sem)
    proj_copy.start()
    for step in range(project_steps):
        sketch_copy(step).start()
    next_copies = []
    if len(spans) > 1:
        next_copies = both_copies(kernel_ref, next_ref, next_sems, spans[1])
    proj_copy.wait()

    def project(step, carry):
        sketch_copy(step).wait()
        both = jnp.concatenate([parts_ref[0], parts_ref[1]], axis=1)
        rows = pl.ds(pl.multiple_of(step * deep, deep), deep)
        for one in range(passes):
            cols = slice(2 * one * rank, 2 * (one + 1) * rank)
            sk_ref[rows, cols] = product(held_ref[one, rows, :], both).astype(jnp.bfloat16)
        return carry

    def gather(part, carry):
        for copy in block_copies(kernel_ref, block_ref, block_sems, spans[0], part):
            copy.wait()

        @pl.when(part == 0)
        def _():
            for copy in next_copies:
                copy.start()

        acc_ref[part] = product(block_ref[part].reshape(-1, cols), sk_ref[...])
        return carry

    for part in range(2):
        lax.fori_loop(part, part + 1, project, 0)
        for copy in block_copies(kernel_ref, block_ref, block_sems, spans[0], part):
            copy.start()
    lax.fori_loop(2, project_steps, project, 0)
    lax.fori_loop(0, 2, gather, 0)
    write_pieces(place_ref[0], acc_ref, keep_ref, send_ref, 0, 0, spans[0][1])
    if len(spans) > 1:
        wait_all(kernel_ref, next_ref, next_sems, spans[1])


def cost_of(kernel, span, width):
    _, segments, _, cols = kernel.shape
    return pl.CostEstimate(
        flops=4 * segments * span[1] * cols * width,
        bytes_accessed=4 * segments * span[1] * cols,
        transcendentals=0,
    )


def first_gathered(place, kernel, sketch, projections, spans, chunk_rows):
    _, segments, _, cols = kernel.shape
    passes, _, sketch_cols = sketch.shape
    rank = projections.shape[4]
    width = 2 * passes * rank
    piece = pltpu.VMEM((segments // 2, passes, chunk_rows, 2 * rank), jnp.bfloat16)
    out_shape = [piece, piece, pltpu.VMEM((cols, width), jnp.bfloat16)]
    scratch = [
        pltpu.VMEM(sketch.shape, sketch.dtype),
        pltpu.VMEM((2, sketch_cols, rank), projections.dtype),
        pltpu.VMEM((2, segments, spans[0][1], cols), kernel.dtype),
        pltpu.VMEM((2, segments * spans[0][1], width), jnp.float32),
        pltpu.SemaphoreType.DMA((project_steps,)),
        pltpu.SemaphoreType.DMA(()),
        pltpu.SemaphoreType.DMA((2, segments)),
    ]
    if len(spans) > 1:
        out_shape.append(pltpu.VMEM((2, segments, spans[1][1], cols), kernel.dtype))
        scratch.append(pltpu.SemaphoreType.DMA((2, segments)))
    return pl.pallas_call(
        functools.partial(first_body, spans=spans),
        name="gather_first",
        in_specs=[in_smem, in_hbm, in_hbm, in_hbm],
        out_specs=[in_vmem] * len(out_shape),
        out_shape=out_shape,
        scratch_shapes=scratch,
        compiler_params=params(28),
        cost_estimate=cost_of(kernel, spans[0], width),
    )(place, remote(kernel), remote(sketch), remote(projections))


def wait_all(kernel_ref, block_ref, sems, span):
    def part_wait(part, carry):
        for copy in block_copies(kernel_ref, block_ref, sems, span, part):
            copy.wait()
        return carry

    lax.fori_loop(0, 2, part_wait, 0)


def start_all(kernel_ref, block_ref, sems, span):
    def part_start(part, carry):
        for copy in block_copies(kernel_ref, block_ref, sems, span, part):
            copy.start()
        return carry

    lax.fori_loop(0, 2, part_start, 0)


def gather_body(place_ref, block_ref, sk_ref, *rest, chunk, first, next_span, filled):
    rest = list(rest)
    if next_span is not None:
        kernel_ref = rest.pop(0)
    if filled:
        del rest[:2]
    keep_ref, send_ref, *rest = rest
    if next_span is not None:
        next_ref, acc_ref, sems = rest
        start_all(kernel_ref, next_ref, sems, next_span)
    else:
        (acc_ref,) = rest
    rows, cols = block_ref.shape[2:]
    both = product(block_ref[...].reshape(-1, cols), sk_ref[...])
    acc_ref[...] = both.reshape(acc_ref.shape)
    write_pieces(place_ref[0], acc_ref, keep_ref, send_ref, chunk, first, rows)
    if next_span is not None:
        wait_all(kernel_ref, next_ref, sems, next_span)


def gathered(place, block, sk_value, kernel, passes, chunk, first, chunk_rows, next_span, partly):
    _, segments, rows, cols = block.shape
    width = sk_value.shape[1]
    piece = pltpu.VMEM((segments // 2, passes, chunk_rows, width // passes), jnp.bfloat16)
    operands = [place, local(block), local(sk_value)]
    in_specs = [in_smem, in_vmem, in_vmem]
    out_shape = [piece, piece]
    scratch = [pltpu.VMEM((2, segments * rows, width), jnp.float32)]
    aliases = {}
    if next_span is not None:
        operands.append(remote(kernel))
        in_specs.append(in_hbm)
        out_shape.append(pltpu.VMEM((2, segments, next_span[1], cols), jnp.bfloat16))
        scratch.append(pltpu.SemaphoreType.DMA((2, segments)))
    if partly is not None:
        aliases = {len(operands): 0, len(operands) + 1: 1}
        operands.extend(map(local, partly))
        in_specs.extend([in_vmem, in_vmem])
    return pl.pallas_call(
        functools.partial(
            gather_body, chunk=chunk, first=first, next_span=next_span, filled=partly is not None
        ),
        name="gather",
        in_specs=in_specs,
        out_specs=[in_vmem] * len(out_shape),
        out_shape=out_shape,
        scratch_shapes=scratch,
        input_output_aliases=aliases,
        compiler_params=params(12),
        cost_estimate=cost_of(kernel, (0, rows), width),
    )(*operands)


def sum_body(*refs, stages):
    for held, got, got_row, hold, send, send_row, own in stages:
        total = refs[held][...].astype(jnp.float32)
        width = total.shape[3]
        if got_row is None:
            total = total + refs[got][...].astype(jnp.float32)
        else:
            rows = total.size // width
            total = total + refs[got][got_row : got_row + rows, :].astype(jnp.float32).reshape(total.shape)
        half = total.shape[0] // 2
        if own is None:
            flat = total[half:].astype(jnp.bfloat16).reshape(-1, width)
            refs[hold][...] = total[:half]
            refs[send][send_row : send_row + flat.shape[0], :] = flat
        else:
            refs[own][...] = total[0].astype(jnp.bfloat16)


def summed(parts, count):
    operands = []
    out_shape = []
    entries = []
    send_row = 0
    for phase, held, got, got_row in parts:
        pieces = 1 << (count - phase)
        passes, chunk_rows, width = held.shape[1:]
        entry = [len(operands), len(operands) + 1, got_row, None, None, None, None]
        operands.extend([local(held), local(got)])
        if phase == count:
            entry[6] = len(out_shape)
            out_shape.append(pltpu.VMEM((passes, chunk_rows, width), jnp.bfloat16))
        else:
            entry[3] = len(out_shape)
            entry[5] = send_row
            send_row += passes * chunk_rows * (pieces // 2)
            out_shape.append(pltpu.VMEM((pieces // 2, passes, chunk_rows, width), jnp.float32))
        entries.append(entry)
    if send_row:
        out_shape.append(pltpu.VMEM((send_row, width), jnp.bfloat16))
    for entry in entries:
        if entry[6] is None:
            entry[3] += len(operands)
            entry[4] = len(operands) + len(out_shape) - 1
        else:
            entry[6] += len(operands)
    results = pl.pallas_call(
        functools.partial(sum_body, stages=tuple(map(tuple, entries))),
        name="sum_parts",
        in_specs=[in_vmem] * len(operands),
        out_specs=[in_vmem] * len(out_shape),
        out_shape=out_shape,
        compiler_params=params(8),
    )(*operands)
    return results


def plan_of(count):
    if count == 2:
        return exchanges
    chunks = len(shares)
    return tuple(
        tuple((step - phase, phase) for phase in range(count) if 0 <= step - phase < chunks)
        for step in range(chunks + count - 1)
    )


def weights_body(proj_ref, inv_ref, *out_refs):
    levels = proj_ref.shape[0]
    rank = proj_ref.shape[4]
    for level in range(levels):
        for half in range(2):
            rows = slice(half * rank, (half + 1) * rank)
            re = inv_ref[level, 0, 0, rows, :]
            im = inv_ref[level, 0, 1, rows, :]
            if level + 1 < levels:
                next_re = proj_ref[level + 1, 0, 0]
                next_im = proj_ref[level + 1, 0, 1]
                re, im = (
                    (product(re, next_re) - product(im, next_im)).astype(jnp.bfloat16),
                    (product(re, next_im) + product(im, next_re)).astype(jnp.bfloat16),
                )
            cols = re.shape[1]
            out_refs[level][half * 2 * rank : half * 2 * rank + rank, :cols] = re
            out_refs[level][half * 2 * rank : half * 2 * rank + rank, cols:] = im
            out_refs[level][half * 2 * rank + rank : (half + 1) * 2 * rank, :cols] = -im
            out_refs[level][half * 2 * rank + rank : (half + 1) * 2 * rank, cols:] = re


def level_weights(projections, inverses):
    levels = projections.shape[0]
    rank = projections.shape[4]
    sketch_cols = inverses.shape[4]
    shapes = [
        pltpu.VMEM((4 * rank, 2 * (rank if level + 1 < levels else sketch_cols)), jnp.bfloat16)
        for level in range(levels)
    ]
    return pl.pallas_call(
        weights_body,
        name="level_weights",
        out_specs=[in_vmem] * levels,
        out_shape=shapes,
        compiler_params=params(8),
    )(projections, inverses)


def paired(own, partner, weight_ref):
    width = own.shape[-1]
    own = own.reshape(-1, width)
    partner = partner.reshape(-1, width)
    return product(own, weight_ref[:width, :]) + product(partner, weight_ref[width:, :])


def middle_body(*refs, count):
    weight_ref = refs[2 * count]
    out_ref = refs[2 * count + 1]
    first = 0
    for place in range(count):
        own = refs[place][...]
        rows = own.shape[1]
        value = paired(own, refs[count + place][...], weight_ref)
        out_ref[:, first : first + rows, :] = value.astype(jnp.bfloat16).reshape(own.shape)
        first += rows


def middle_level(owns, partners, weight):
    passes, _, width = owns[0].shape
    rows = sum(own.shape[1] for own in owns)
    operands = [local(value) for value in (*owns, *partners, weight)]
    return pl.pallas_call(
        functools.partial(middle_body, count=len(owns)),
        name="middle_level",
        in_specs=[in_vmem] * len(operands),
        out_specs=in_vmem,
        out_shape=pltpu.VMEM((passes, rows, width), jnp.bfloat16),
        compiler_params=params(4),
    )(*operands)


def normalized(own_ref, partner_ref, weight_ref, gain_ref):
    current = paired(own_ref[...], partner_ref[...], weight_ref)
    sketch_cols = gain_ref.shape[1]
    power = jnp.sum(current * current, axis=-1, keepdims=True) / sketch_cols
    scale = lax.rsqrt(power + epsilon)
    gain = gain_ref[...]
    shape = own_ref.shape[:2] + (sketch_cols,)
    return (
        (current[:, :sketch_cols] * scale * gain).reshape(shape),
        (current[:, sketch_cols:] * scale * gain).reshape(shape),
    )


def staged_body(own_ref, partner_ref, weight_ref, gain_ref, stage_ref):
    stage_ref[0], stage_ref[1] = normalized(own_ref, partner_ref, weight_ref, gain_ref)


def staged_level(own, partner, weight, gain):
    passes, rows, _ = own.shape
    return pl.pallas_call(
        staged_body,
        name="staged_level",
        in_specs=[in_vmem] * 4,
        out_specs=in_vmem,
        out_shape=pltpu.VMEM((2, passes, rows, gain.shape[1]), jnp.float32),
        compiler_params=params(8),
    )(local(own), local(partner), local(weight), local(gain))


def final_body(own_ref, partner_ref, weight_ref, gain_ref, *rest, firsts):
    stages = rest[: len(firsts) - 1]
    out_ref, stage_ref, sems = rest[len(firsts) - 1 :]
    copies = []
    for place, (first, part_ref) in enumerate(zip(firsts, (*stages, stage_ref))):
        target = out_ref.at[:, :, pl.ds(first, part_ref.shape[2]), :]
        copies.append(pltpu.make_async_copy(part_ref, target, sems.at[place]))
    for copy in copies[:-1]:
        copy.start()
    stage_ref[0], stage_ref[1] = normalized(own_ref, partner_ref, weight_ref, gain_ref)
    copies[-1].start()
    for copy in copies:
        copy.wait()


def final_level(own, partner, weight, gain, stages, firsts, segment_rows):
    passes, rows, _ = own.shape
    sketch_cols = gain.shape[1]
    operands = [local(value) for value in (own, partner, weight, gain, *stages)]
    return pl.pallas_call(
        functools.partial(final_body, firsts=tuple(firsts)),
        name="final_level",
        in_specs=[in_vmem] * len(operands),
        out_specs=in_hbm,
        out_shape=jax.ShapeDtypeStruct((2, passes, segment_rows, sketch_cols), jnp.float32),
        scratch_shapes=[
            pltpu.VMEM((2, passes, rows, sketch_cols), jnp.float32),
            pltpu.SemaphoreType.DMA((len(firsts),)),
        ],
        compiler_params=params(8),
    )(*operands)


def shards(kernel, sketch, projections, inverses, norm_gain):
    members = lax.axis_size("sk")
    count = phase_count(members)
    levels = projections.shape[0]
    passes = sketch.shape[0]
    top_bits = lax.axis_size("bf").bit_length() - 1
    _, rows, cols = kernel.shape
    segment_rows = rows // members
    unit = segment_rows // sum(shares)
    spans = []
    for share in shares:
        first = spans[-1][0] + spans[-1][1] if spans else 0
        spans.append((first, share * unit))
    chunks = len(spans)
    kernel = kernel.reshape(2, members, segment_rows, cols)
    place = lax.axis_index("sk").reshape(1).astype(jnp.int32)
    gain = norm_gain.reshape(1, -1)
    weights = level_weights(projections, inverses)
    keeps = []
    cores = []
    block = None
    pieces = []
    for chunk, span in enumerate(spans):
        rows = span[1] // splits[chunk]
        pieces.extend((chunk, part * rows, (span[0] + part * rows, rows)) for part in range(splits[chunk]))
    filled = None
    for number, (chunk, first, span) in enumerate(pieces):
        next_span = pieces[number + 1][2] if number + 1 < len(pieces) else None
        chunk_rows = spans[chunk][1]
        if number == 0:
            both = [span] if next_span is None else [span, next_span]
            keep, send, sk_value, *blocks = first_gathered(
                place, kernel, sketch, projections, both, chunk_rows
            )
        else:
            keep, send, *blocks = gathered(
                place, block, sk_value, kernel, passes, chunk, first, chunk_rows, next_span, filled
            )
        filled = (keep, send)
        if blocks:
            block = blocks[0]
        if first + span[1] == chunk_rows:
            filled = None
            keeps.append(keep)
            cores.append(swapped(send, "sk", 1))
    held = dict(enumerate(keeps))
    got = {chunk: (core, None) for chunk, core in enumerate(cores)}
    for place, exchange in enumerate(plan_of(count)):
        parts = [(phase, held[chunk], *got[chunk]) for chunk, phase in exchange]
        *kept, send = summed(parts, count)
        chunk, phase = exchange[0]
        received = swapped_step(send, chunk + phase)
        row = 0
        for (chunk, _), value in zip(exchange, kept):
            held[chunk] = value
            got[chunk] = (received, row)
            row += value.size // value.shape[3]
    owns = []
    for chunk in range(chunks):
        owns.extend(summed([(count, held[chunk], *got[chunk])], count))
    partners = []
    for chunk in range(chunks):
        partners.append(swapped(owns[chunk], "bf", 2 ** (top_bits - 1)))
    stages = []
    firsts = []
    for place, group in enumerate(groups):
        own = [owns[chunk] for chunk in group]
        partner = [partners[chunk] for chunk in group]
        for level in range(1, levels):
            merged = middle_level(own, partner, weights[level - 1])
            own = [merged]
            partner = [swapped(merged, "bf", 2 ** (top_bits - 1 - level))]
        firsts.append(spans[group[0]][0])
        if place + 1 < len(groups):
            stages.append(staged_level(own[0], partner[0], weights[levels - 1], gain))
        else:
            out = final_level(
                own[0], partner[0], weights[levels - 1], gain, stages, firsts, segment_rows
            )
    return out


def solution(mesh):
    placed = (
        P(None, "bf", "sk"),
        P(None, "sk", None),
        P(None, "bf", None, None, None),
        P(None, "bf", None, None, None),
        P(),
    )

    return jax.shard_map(
        shards,
        mesh=mesh,
        in_specs=placed,
        out_specs=P(None, None, ("bf", "sk"), None),
        check_vma=False,
    )
```

```python
import functools
import jax
import jax.numpy as jnp
from jax import lax
from jax.experimental import pallas as pl
from jax.experimental.pallas import tpu as pltpu
from jax.sharding import PartitionSpec as P

epsilon = 1e-06
shares = (2, 2, 2, 2)
splits = (1, 1, 1, 1)
groups = ((0,), (1,), (2,), (3,))
exchanges = (((0, 0),), ((0, 1), (1, 0)), ((1, 1),), ((2, 0),), ((2, 1),), ((3, 0),), ((3, 1),))
project_steps = 2
row_tile = 16
mib = 1024 * 1024
in_vmem = pl.BlockSpec(memory_space=pltpu.VMEM)
in_hbm = pl.BlockSpec(memory_space=pltpu.HBM)
in_smem = pl.BlockSpec(memory_space=pltpu.SMEM)


def swapped(value, axis, mask):
    pairs = [(source, source ^ mask) for source in range(lax.axis_size(axis))]
    return lax.ppermute(value, axis, pairs)


def phase_count(members):
    return members.bit_length() - 2


def chip_bit(core, step, count):
    return (core + step) % count


def swapped_step(value, step):
    members = lax.axis_size("sk")
    count = phase_count(members)
    pairs = [
        (source, source ^ (2 << chip_bit(source % 2, step, count))) for source in range(members)
    ]
    return lax.ppermute(value, "sk", pairs)


def product(left, right):
    return lax.dot_general(left, right, (((1,), (0,)), ((), ())), preferred_element_type=jnp.float32)


def params(megabytes):
    return pltpu.CompilerParams(vmem_limit_bytes=megabytes * mib)


def local(value):
    return pltpu.with_memory_space_constraint(value, pltpu.VMEM)


def remote(value):
    return pltpu.with_memory_space_constraint(value, pltpu.HBM)


def piece_target(place, index, segments, chunk):
    count = phase_count(segments)
    turns = []
    for core in range(2):
        turn = 0
        for phase in range(count):
            if (index >> (count - 1 - phase)) & 1:
                turn |= 2 << chip_bit(core, chunk + phase, count)
        turns.append(turn)
    return place ^ jnp.where(place % 2 == 0, turns[0], turns[1])


def write_pieces(place, acc_ref, keep_ref, send_ref, chunk, first, chunk_rows, one):
    halves = keep_ref.shape[0]
    rank = keep_ref.shape[3] // 2
    segments = 2 * halves
    kept = slice(first, first + chunk_rows)
    for turn in range(segments):
        out_ref = send_ref if turn % 2 else keep_ref
        target = piece_target(place ^ (turn % 2), turn // 2, segments, chunk)
        rows = pl.ds(pl.multiple_of(target * chunk_rows, chunk_rows), chunk_rows)
        upper = acc_ref[0, rows, :]
        lower = acc_ref[1, rows, :]
        out_ref[turn // 2, one, kept, :rank] = (upper[:, :rank] - lower[:, rank:]).astype(jnp.bfloat16)
        out_ref[turn // 2, one, kept, rank:] = (upper[:, rank:] + lower[:, :rank]).astype(jnp.bfloat16)


def gather_passes(place, block_ref, sk_ref, acc_refs, keep_ref, send_ref, chunk, first):
    rows, cols = block_ref.shape[2:]
    width = keep_ref.shape[3]
    for one, acc_ref in enumerate(acc_refs):
        part = sk_ref[:, one * width : (one + 1) * width]
        both = product(block_ref[...].reshape(-1, cols), part)
        acc_ref[...] = both.reshape(acc_ref.shape)
        write_pieces(place, acc_ref, keep_ref, send_ref, chunk, first, rows, one)


def block_copies(kernel_ref, block_ref, sems, span, part):
    return [
        pltpu.make_async_copy(
            kernel_ref.at[part, segment, pl.ds(*span), :],
            block_ref.at[part, segment],
            sems.at[part, segment],
        )
        for segment in range(block_ref.shape[1])
    ]


def wait_all(kernel_ref, block_ref, sems, span):
    def part_wait(part, carry):
        for copy in block_copies(kernel_ref, block_ref, sems, span, part):
            copy.wait()
        return carry

    lax.fori_loop(0, 2, part_wait, 0)


def start_all(kernel_ref, block_ref, sems, span):
    def part_start(part, carry):
        for copy in block_copies(kernel_ref, block_ref, sems, span, part):
            copy.start()
        return carry

    lax.fori_loop(0, 2, part_start, 0)


def first_body(place_ref, kernel_ref, sketch_ref, proj_ref, *rest, spans):
    if len(spans) > 1:
        keep_ref, send_ref, sk_ref, next_ref, *rest = rest
        *rest, next_sems = rest
    else:
        keep_ref, send_ref, sk_ref, *rest = rest
    held_ref, parts_ref, block_ref, *acc_refs, sketch_sems, proj_sem, block_sems = rest
    passes, cols, _ = sketch_ref.shape
    rank = proj_ref.shape[4]
    deep = cols // project_steps

    def sketch_copy(step):
        rows = pl.ds(pl.multiple_of(step * deep, deep), deep)
        return pltpu.make_async_copy(
            sketch_ref.at[:, rows, :], held_ref.at[:, rows, :], sketch_sems.at[step]
        )

    proj_copy = pltpu.make_async_copy(proj_ref.at[0, 0], parts_ref, proj_sem)
    proj_copy.start()
    for step in range(project_steps):
        sketch_copy(step).start()
    proj_copy.wait()

    def project(step, carry):
        sketch_copy(step).wait()
        both = jnp.concatenate([parts_ref[0], parts_ref[1]], axis=1)
        rows = pl.ds(pl.multiple_of(step * deep, deep), deep)
        for one in range(passes):
            cols = slice(2 * one * rank, 2 * (one + 1) * rank)
            sk_ref[rows, cols] = product(held_ref[one, rows, :], both).astype(jnp.bfloat16)
        return carry

    for part in range(2):
        lax.fori_loop(part, part + 1, project, 0)
        for copy in block_copies(kernel_ref, block_ref, block_sems, spans[0], part):
            copy.start()
    lax.fori_loop(2, project_steps, project, 0)
    width = 2 * rank

    next_copies = []
    if len(spans) > 1:
        for part in range(2):
            next_copies.extend(block_copies(kernel_ref, next_ref, next_sems, spans[1], part))

    def gather(part, carry):
        for copy in block_copies(kernel_ref, block_ref, block_sems, spans[0], part):
            copy.wait()

        @pl.when(part == 0)
        def _():
            for copy in next_copies:
                copy.start()

        both = product(block_ref[part].reshape(-1, cols), sk_ref[...])
        for one, acc_ref in enumerate(acc_refs):
            acc_ref[part] = both[:, one * width : (one + 1) * width]
        return carry

    lax.fori_loop(0, 2, gather, 0)
    for one, acc_ref in enumerate(acc_refs):
        write_pieces(place_ref[0], acc_ref, keep_ref, send_ref, 0, 0, spans[0][1], one)
    if len(spans) > 1:
        wait_all(kernel_ref, next_ref, next_sems, spans[1])


def cost_of(kernel, span, width):
    _, segments, _, cols = kernel.shape
    return pl.CostEstimate(
        flops=4 * segments * span[1] * cols * width,
        bytes_accessed=4 * segments * span[1] * cols,
        transcendentals=0,
    )


def first_gathered(place, kernel, sketch, projections, spans, chunk_rows):
    _, segments, _, cols = kernel.shape
    passes, _, sketch_cols = sketch.shape
    rank = projections.shape[4]
    width = 2 * passes * rank
    piece = pltpu.VMEM((segments // 2, passes, chunk_rows, 2 * rank), jnp.bfloat16)
    out_shape = [piece, piece, pltpu.VMEM((cols, width), jnp.bfloat16)]
    scratch = [
        pltpu.VMEM(sketch.shape, sketch.dtype),
        pltpu.VMEM((2, sketch_cols, rank), projections.dtype),
        pltpu.VMEM((2, segments, spans[0][1], cols), kernel.dtype),
        *[pltpu.VMEM((2, segments * spans[0][1], 2 * rank), jnp.float32)] * passes,
        pltpu.SemaphoreType.DMA((project_steps,)),
        pltpu.SemaphoreType.DMA(()),
        pltpu.SemaphoreType.DMA((2, segments)),
    ]
    if len(spans) > 1:
        out_shape.append(pltpu.VMEM((2, segments, spans[1][1], cols), kernel.dtype))
        scratch.append(pltpu.SemaphoreType.DMA((2, segments)))
    return pl.pallas_call(
        functools.partial(first_body, spans=spans),
        name="gather_first",
        in_specs=[in_smem, in_hbm, in_hbm, in_hbm],
        out_specs=[in_vmem] * len(out_shape),
        out_shape=out_shape,
        scratch_shapes=scratch,
        compiler_params=params(28),
        cost_estimate=cost_of(kernel, spans[0], width),
    )(place, remote(kernel), remote(sketch), remote(projections))


def gather_body(place_ref, block_ref, sk_ref, *rest, chunk, first, next_span, filled):
    rest = list(rest)
    if next_span is not None:
        kernel_ref = rest.pop(0)
    if filled:
        del rest[:2]
    keep_ref, send_ref, *rest = rest
    acc_refs = rest
    if next_span is not None:
        next_ref, *acc_refs, sems = rest
        start_all(kernel_ref, next_ref, sems, next_span)
    gather_passes(place_ref[0], block_ref, sk_ref, acc_refs, keep_ref, send_ref, chunk, first)
    if next_span is not None:
        wait_all(kernel_ref, next_ref, sems, next_span)


def gathered(place, block, sk_value, kernel, passes, chunk, first, chunk_rows, next_span, partly):
    _, segments, rows, cols = block.shape
    width = sk_value.shape[1]
    piece = pltpu.VMEM((segments // 2, passes, chunk_rows, width // passes), jnp.bfloat16)
    operands = [place, local(block), local(sk_value)]
    in_specs = [in_smem, in_vmem, in_vmem]
    out_shape = [piece, piece]
    scratch = [pltpu.VMEM((2, segments * rows, width // passes), jnp.float32)] * passes
    aliases = {}
    if next_span is not None:
        operands.append(remote(kernel))
        in_specs.append(in_hbm)
        out_shape.append(pltpu.VMEM((2, segments, next_span[1], cols), jnp.bfloat16))
        scratch.append(pltpu.SemaphoreType.DMA((2, segments)))
    if partly is not None:
        aliases = {len(operands): 0, len(operands) + 1: 1}
        operands.extend(map(local, partly))
        in_specs.extend([in_vmem, in_vmem])
    return pl.pallas_call(
        functools.partial(
            gather_body, chunk=chunk, first=first, next_span=next_span, filled=partly is not None
        ),
        name="gather",
        in_specs=in_specs,
        out_specs=[in_vmem] * len(out_shape),
        out_shape=out_shape,
        scratch_shapes=scratch,
        input_output_aliases=aliases,
        compiler_params=params(12),
        cost_estimate=cost_of(kernel, (0, rows), width),
    )(*operands)


def sum_body(*refs, stages):
    for held, got, got_row, hold, send, send_row, own in stages:
        total = refs[held][...].astype(jnp.float32)
        width = total.shape[3]
        if got_row is None:
            total = total + refs[got][...].astype(jnp.float32)
        else:
            rows = total.size // width
            total = total + refs[got][got_row : got_row + rows, :].astype(jnp.float32).reshape(total.shape)
        half = total.shape[0] // 2
        if own is None:
            flat = total[half:].astype(jnp.bfloat16).reshape(-1, width)
            refs[hold][...] = total[:half]
            refs[send][send_row : send_row + flat.shape[0], :] = flat
        else:
            refs[own][...] = total[0].astype(jnp.bfloat16)


def summed(parts, count):
    operands = []
    out_shape = []
    entries = []
    send_row = 0
    for phase, held, got, got_row in parts:
        pieces = 1 << (count - phase)
        passes, chunk_rows, width = held.shape[1:]
        entry = [len(operands), len(operands) + 1, got_row, None, None, None, None]
        operands.extend([local(held), local(got)])
        if phase == count:
            entry[6] = len(out_shape)
            out_shape.append(pltpu.VMEM((passes, chunk_rows, width), jnp.bfloat16))
        else:
            entry[3] = len(out_shape)
            entry[5] = send_row
            send_row += passes * chunk_rows * (pieces // 2)
            out_shape.append(pltpu.VMEM((pieces // 2, passes, chunk_rows, width), jnp.float32))
        entries.append(entry)
    if send_row:
        out_shape.append(pltpu.VMEM((send_row, width), jnp.bfloat16))
    for entry in entries:
        if entry[6] is None:
            entry[3] += len(operands)
            entry[4] = len(operands) + len(out_shape) - 1
        else:
            entry[6] += len(operands)
    results = pl.pallas_call(
        functools.partial(sum_body, stages=tuple(map(tuple, entries))),
        name="sum_parts",
        in_specs=[in_vmem] * len(operands),
        out_specs=[in_vmem] * len(out_shape),
        out_shape=out_shape,
        compiler_params=params(8),
    )(*operands)
    return results


def plan_of(count):
    if count == 2:
        return exchanges
    chunks = len(shares)
    return tuple(
        tuple((step - phase, phase) for phase in range(count) if 0 <= step - phase < chunks)
        for step in range(chunks + count - 1)
    )


def weights_body(proj_ref, inv_ref, *out_refs):
    levels = proj_ref.shape[0]
    rank = proj_ref.shape[4]
    for level in range(levels):
        for half in range(2):
            rows = slice(half * rank, (half + 1) * rank)
            re = inv_ref[level, 0, 0, rows, :]
            im = inv_ref[level, 0, 1, rows, :]
            if level + 1 < levels:
                next_re = proj_ref[level + 1, 0, 0]
                next_im = proj_ref[level + 1, 0, 1]
                re, im = (
                    (product(re, next_re) - product(im, next_im)).astype(jnp.bfloat16),
                    (product(re, next_im) + product(im, next_re)).astype(jnp.bfloat16),
                )
            cols = re.shape[1]
            out_refs[level][half * 2 * rank : half * 2 * rank + rank, :cols] = re
            out_refs[level][half * 2 * rank : half * 2 * rank + rank, cols:] = im
            out_refs[level][half * 2 * rank + rank : (half + 1) * 2 * rank, :cols] = -im
            out_refs[level][half * 2 * rank + rank : (half + 1) * 2 * rank, cols:] = re


def level_weights(projections, inverses):
    levels = projections.shape[0]
    rank = projections.shape[4]
    sketch_cols = inverses.shape[4]
    shapes = [
        pltpu.VMEM((4 * rank, 2 * (rank if level + 1 < levels else sketch_cols)), jnp.bfloat16)
        for level in range(levels)
    ]
    return pl.pallas_call(
        weights_body,
        name="level_weights",
        out_specs=[in_vmem] * levels,
        out_shape=shapes,
        compiler_params=params(8),
    )(projections, inverses)


def paired(own, partner, weight_ref):
    width = own.shape[-1]
    own = own.reshape(-1, width)
    partner = partner.reshape(-1, width)
    return product(own, weight_ref[:width, :]) + product(partner, weight_ref[width:, :])


def middle_body(*refs, count):
    weight_ref = refs[2 * count]
    out_ref = refs[2 * count + 1]
    first = 0
    for place in range(count):
        own = refs[place][...]
        rows = own.shape[1]
        value = paired(own, refs[count + place][...], weight_ref)
        out_ref[:, first : first + rows, :] = value.astype(jnp.bfloat16).reshape(own.shape)
        first += rows


def middle_level(owns, partners, weight):
    passes, _, width = owns[0].shape
    rows = sum(own.shape[1] for own in owns)
    operands = [local(value) for value in (*owns, *partners, weight)]
    return pl.pallas_call(
        functools.partial(middle_body, count=len(owns)),
        name="middle_level",
        in_specs=[in_vmem] * len(operands),
        out_specs=in_vmem,
        out_shape=pltpu.VMEM((passes, rows, width), jnp.bfloat16),
        compiler_params=params(4),
    )(*operands)


def normalized(own_ref, partner_ref, weight_ref, gain_ref):
    current = paired(own_ref[...], partner_ref[...], weight_ref)
    sketch_cols = gain_ref.shape[1]
    power = jnp.sum(current * current, axis=-1, keepdims=True) / sketch_cols
    scale = lax.rsqrt(power + epsilon)
    gain = gain_ref[...]
    shape = own_ref.shape[:2] + (sketch_cols,)
    return (
        (current[:, :sketch_cols] * scale * gain).reshape(shape),
        (current[:, sketch_cols:] * scale * gain).reshape(shape),
    )


def staged_body(own_ref, partner_ref, weight_ref, gain_ref, stage_ref):
    stage_ref[0], stage_ref[1] = normalized(own_ref, partner_ref, weight_ref, gain_ref)


def staged_level(own, partner, weight, gain):
    passes, rows, _ = own.shape
    return pl.pallas_call(
        staged_body,
        name="staged_level",
        in_specs=[in_vmem] * 4,
        out_specs=in_vmem,
        out_shape=pltpu.VMEM((2, passes, rows, gain.shape[1]), jnp.float32),
        compiler_params=params(8),
    )(local(own), local(partner), local(weight), local(gain))


def final_body(own_ref, partner_ref, weight_ref, gain_ref, *rest, firsts):
    stages = rest[: len(firsts) - 1]
    out_ref, stage_ref, sems = rest[len(firsts) - 1 :]
    copies = []
    for place, (first, part_ref) in enumerate(zip(firsts, (*stages, stage_ref))):
        target = out_ref.at[:, :, pl.ds(first, part_ref.shape[2]), :]
        copies.append(pltpu.make_async_copy(part_ref, target, sems.at[place]))
    for copy in copies[:-1]:
        copy.start()
    stage_ref[0], stage_ref[1] = normalized(own_ref, partner_ref, weight_ref, gain_ref)
    copies[-1].start()
    for copy in copies:
        copy.wait()


def final_level(own, partner, weight, gain, stages, firsts, segment_rows):
    passes, rows, _ = own.shape
    sketch_cols = gain.shape[1]
    operands = [local(value) for value in (own, partner, weight, gain, *stages)]
    return pl.pallas_call(
        functools.partial(final_body, firsts=tuple(firsts)),
        name="final_level",
        in_specs=[in_vmem] * len(operands),
        out_specs=in_hbm,
        out_shape=jax.ShapeDtypeStruct((2, passes, segment_rows, sketch_cols), jnp.float32),
        scratch_shapes=[
            pltpu.VMEM((2, passes, rows, sketch_cols), jnp.float32),
            pltpu.SemaphoreType.DMA((len(firsts),)),
        ],
        compiler_params=params(8),
    )(*operands)


def shards(kernel, sketch, projections, inverses, norm_gain):
    members = lax.axis_size("sk")
    count = phase_count(members)
    levels = projections.shape[0]
    passes = sketch.shape[0]
    top_bits = lax.axis_size("bf").bit_length() - 1
    _, rows, cols = kernel.shape
    segment_rows = rows // members
    tiles = segment_rows // row_tile
    bounds = [tiles * sum(shares[:end]) // sum(shares) * row_tile for end in range(len(shares) + 1)]
    spans = [(first, last - first) for first, last in zip(bounds, bounds[1:])]
    chunks = len(spans)
    kernel = kernel.reshape(2, members, segment_rows, cols)
    place = lax.axis_index("sk").reshape(1).astype(jnp.int32)
    gain = norm_gain.reshape(1, -1)
    weights = level_weights(projections, inverses)
    keeps = []
    cores = []
    block = None
    pieces = []
    for chunk, span in enumerate(spans):
        rows = span[1] // splits[chunk]
        pieces.extend((chunk, part * rows, (span[0] + part * rows, rows)) for part in range(splits[chunk]))
    filled = None
    for number, (chunk, first, span) in enumerate(pieces):
        next_span = pieces[number + 1][2] if number + 1 < len(pieces) else None
        chunk_rows = spans[chunk][1]
        if number == 0:
            both = [span] if next_span is None else [span, next_span]
            keep, send, sk_value, *blocks = first_gathered(
                place, kernel, sketch, projections, both, chunk_rows
            )
        else:
            keep, send, *blocks = gathered(
                place, block, sk_value, kernel, passes, chunk, first, chunk_rows, next_span, filled
            )
        filled = (keep, send)
        if blocks:
            block = blocks[0]
        if first + span[1] == chunk_rows:
            filled = None
            keeps.append(keep)
            cores.append(swapped(send, "sk", 1))
    held = dict(enumerate(keeps))
    got = {chunk: (core, None) for chunk, core in enumerate(cores)}
    for place, exchange in enumerate(plan_of(count)):
        parts = [(phase, held[chunk], *got[chunk]) for chunk, phase in exchange]
        *kept, send = summed(parts, count)
        chunk, phase = exchange[0]
        received = swapped_step(send, chunk + phase)
        row = 0
        for (chunk, _), value in zip(exchange, kept):
            held[chunk] = value
            got[chunk] = (received, row)
            row += value.size // value.shape[3]
    owns = []
    for chunk in range(chunks):
        owns.extend(summed([(count, held[chunk], *got[chunk])], count))
    partners = []
    for chunk in range(chunks):
        partners.append(swapped(owns[chunk], "bf", 2 ** (top_bits - 1)))
    stages = []
    firsts = []
    for place, group in enumerate(groups):
        own = [owns[chunk] for chunk in group]
        partner = [partners[chunk] for chunk in group]
        for level in range(1, levels):
            merged = middle_level(own, partner, weights[level - 1])
            own = [merged]
            partner = [swapped(merged, "bf", 2 ** (top_bits - 1 - level))]
        firsts.append(spans[group[0]][0])
        if place + 1 < len(groups):
            stages.append(staged_level(own[0], partner[0], weights[levels - 1], gain))
        else:
            out = final_level(
                own[0], partner[0], weights[levels - 1], gain, stages, firsts, segment_rows
            )
    return out


def solution(mesh):
    placed = (
        P(None, "bf", "sk"),
        P(None, "sk", None),
        P(None, "bf", None, None, None),
        P(None, "bf", None, None, None),
        P(),
    )

    return jax.shard_map(
        shards,
        mesh=mesh,
        in_specs=placed,
        out_specs=P(None, None, ("bf", "sk"), None),
        check_vma=False,
    )
```

```python
import functools
import jax
import jax.numpy as jnp
from jax import lax
from jax.experimental import pallas as pl
from jax.experimental.pallas import tpu as pltpu
from jax.sharding import PartitionSpec as P

epsilon = 1e-06
shares = (2, 2, 2, 2)
splits = (1, 1, 1, 1)
groups = ((0,), (1,), (2,), (3,))
exchanges = (((0, 0),), ((0, 1), (1, 0)), ((1, 1),), ((2, 0),), ((2, 1),), ((3, 0),), ((3, 1),))
project_steps = 2
row_tile = 16
mib = 1024 * 1024
in_vmem = pl.BlockSpec(memory_space=pltpu.VMEM)
in_hbm = pl.BlockSpec(memory_space=pltpu.HBM)
in_smem = pl.BlockSpec(memory_space=pltpu.SMEM)


def swapped(value, axis, mask):
    pairs = [(source, source ^ mask) for source in range(lax.axis_size(axis))]
    return lax.ppermute(value, axis, pairs)


def phase_count(members):
    return members.bit_length() - 2


def chip_bit(core, step, count):
    return (core + step) % count


def swapped_step(value, step):
    members = lax.axis_size("sk")
    count = phase_count(members)
    pairs = [
        (source, source ^ (2 << chip_bit(source % 2, step, count))) for source in range(members)
    ]
    return lax.ppermute(value, "sk", pairs)


def product(left, right):
    return lax.dot_general(left, right, (((1,), (0,)), ((), ())), preferred_element_type=jnp.float32)


def params(megabytes):
    return pltpu.CompilerParams(vmem_limit_bytes=megabytes * mib)


def local(value):
    return pltpu.with_memory_space_constraint(value, pltpu.VMEM)


def remote(value):
    return pltpu.with_memory_space_constraint(value, pltpu.HBM)


def piece_target(place, index, segments, chunk):
    count = phase_count(segments)
    turns = []
    for core in range(2):
        turn = 0
        for phase in range(count):
            if (index >> (count - 1 - phase)) & 1:
                turn |= 2 << chip_bit(core, chunk + phase, count)
        turns.append(turn)
    return place ^ jnp.where(place % 2 == 0, turns[0], turns[1])


def write_pieces(place, acc_ref, keep_ref, send_ref, chunk, first, chunk_rows, one):
    halves = keep_ref.shape[0]
    rank = keep_ref.shape[3] // 2
    segments = 2 * halves
    kept = slice(first, first + chunk_rows)
    for turn in range(segments):
        out_ref = send_ref if turn % 2 else keep_ref
        target = piece_target(place ^ (turn % 2), turn // 2, segments, chunk)
        rows = pl.ds(pl.multiple_of(target * chunk_rows, chunk_rows), chunk_rows)
        upper = acc_ref[0, rows, :]
        lower = acc_ref[1, rows, :]
        out_ref[turn // 2, one, kept, :rank] = (upper[:, :rank] - lower[:, rank:]).astype(jnp.bfloat16)
        out_ref[turn // 2, one, kept, rank:] = (upper[:, rank:] + lower[:, :rank]).astype(jnp.bfloat16)


def gather_passes(place, block_ref, sk_ref, acc_refs, keep_ref, send_ref, chunk, first):
    rows, cols = block_ref.shape[2:]
    width = keep_ref.shape[3]
    for one, acc_ref in enumerate(acc_refs):
        part = sk_ref[:, one * width : (one + 1) * width]
        both = product(block_ref[...].reshape(-1, cols), part)
        acc_ref[...] = both.reshape(acc_ref.shape)
        write_pieces(place, acc_ref, keep_ref, send_ref, chunk, first, rows, one)


def block_copies(kernel_ref, block_ref, sems, span, part):
    return [
        pltpu.make_async_copy(
            kernel_ref.at[part, segment, pl.ds(*span), :],
            block_ref.at[part, segment],
            sems.at[part, segment],
        )
        for segment in range(block_ref.shape[1])
    ]


def wait_all(kernel_ref, block_ref, sems, span):
    def part_wait(part, carry):
        for copy in block_copies(kernel_ref, block_ref, sems, span, part):
            copy.wait()
        return carry

    lax.fori_loop(0, 2, part_wait, 0)


def start_all(kernel_ref, block_ref, sems, span):
    def part_start(part, carry):
        for copy in block_copies(kernel_ref, block_ref, sems, span, part):
            copy.start()
        return carry

    lax.fori_loop(0, 2, part_start, 0)


def first_body(place_ref, kernel_ref, sketch_ref, proj_ref, *rest, spans):
    if len(spans) > 1:
        keep_ref, send_ref, sk_ref, next_ref, *rest = rest
        *rest, next_sems = rest
    else:
        keep_ref, send_ref, sk_ref, *rest = rest
    held_ref, parts_ref, block_ref, *acc_refs, sketch_sems, proj_sem, block_sems = rest
    passes, cols, _ = sketch_ref.shape
    rank = proj_ref.shape[4]
    deep = cols // project_steps

    def sketch_copy(step):
        rows = pl.ds(pl.multiple_of(step * deep, deep), deep)
        return pltpu.make_async_copy(
            sketch_ref.at[:, rows, :], held_ref.at[:, rows, :], sketch_sems.at[step]
        )

    proj_copy = pltpu.make_async_copy(proj_ref.at[0, 0], parts_ref, proj_sem)
    proj_copy.start()
    for step in range(project_steps):
        sketch_copy(step).start()
    proj_copy.wait()

    def project(step, carry):
        sketch_copy(step).wait()
        both = jnp.concatenate([parts_ref[0], parts_ref[1]], axis=1)
        rows = pl.ds(pl.multiple_of(step * deep, deep), deep)
        for one in range(passes):
            cols = slice(2 * one * rank, 2 * (one + 1) * rank)
            sk_ref[rows, cols] = product(held_ref[one, rows, :], both).astype(jnp.bfloat16)
        return carry

    for part in range(2):
        lax.fori_loop(part, part + 1, project, 0)
        for copy in block_copies(kernel_ref, block_ref, block_sems, spans[0], part):
            copy.start()
    lax.fori_loop(2, project_steps, project, 0)
    width = 2 * rank

    next_copies = []
    if len(spans) > 1:
        for part in range(2):
            next_copies.extend(block_copies(kernel_ref, next_ref, next_sems, spans[1], part))

    def gather(part, carry):
        for copy in block_copies(kernel_ref, block_ref, block_sems, spans[0], part):
            copy.wait()

        @pl.when(part == 0)
        def _():
            for copy in next_copies:
                copy.start()

        both = product(block_ref[part].reshape(-1, cols), sk_ref[...])
        for one, acc_ref in enumerate(acc_refs):
            acc_ref[part] = both[:, one * width : (one + 1) * width]
        return carry

    lax.fori_loop(0, 2, gather, 0)
    for one, acc_ref in enumerate(acc_refs):
        write_pieces(place_ref[0], acc_ref, keep_ref, send_ref, 0, 0, spans[0][1], one)
    if len(spans) > 1:
        wait_all(kernel_ref, next_ref, next_sems, spans[1])


def cost_of(kernel, span, width):
    _, segments, _, cols = kernel.shape
    return pl.CostEstimate(
        flops=4 * segments * span[1] * cols * width,
        bytes_accessed=4 * segments * span[1] * cols,
        transcendentals=0,
    )


def first_gathered(place, kernel, sketch, projections, spans, chunk_rows):
    _, segments, _, cols = kernel.shape
    passes, _, sketch_cols = sketch.shape
    rank = projections.shape[4]
    width = 2 * passes * rank
    piece = pltpu.VMEM((segments // 2, passes, chunk_rows, 2 * rank), jnp.bfloat16)
    out_shape = [piece, piece, pltpu.VMEM((cols, width), jnp.bfloat16)]
    scratch = [
        pltpu.VMEM(sketch.shape, sketch.dtype),
        pltpu.VMEM((2, sketch_cols, rank), projections.dtype),
        pltpu.VMEM((2, segments, spans[0][1], cols), kernel.dtype),
        *[pltpu.VMEM((2, segments * spans[0][1], 2 * rank), jnp.float32)] * passes,
        pltpu.SemaphoreType.DMA((project_steps,)),
        pltpu.SemaphoreType.DMA(()),
        pltpu.SemaphoreType.DMA((2, segments)),
    ]
    if len(spans) > 1:
        out_shape.append(pltpu.VMEM((2, segments, spans[1][1], cols), kernel.dtype))
        scratch.append(pltpu.SemaphoreType.DMA((2, segments)))
    return pl.pallas_call(
        functools.partial(first_body, spans=spans),
        name="gather_first",
        in_specs=[in_smem, in_hbm, in_hbm, in_hbm],
        out_specs=[in_vmem] * len(out_shape),
        out_shape=out_shape,
        scratch_shapes=scratch,
        compiler_params=params(28),
        cost_estimate=cost_of(kernel, spans[0], width),
    )(place, remote(kernel), remote(sketch), remote(projections))


def gather_body(place_ref, block_ref, sk_ref, *rest, chunk, first, next_span, filled):
    rest = list(rest)
    if next_span is not None:
        kernel_ref = rest.pop(0)
    if filled:
        del rest[:2]
    keep_ref, send_ref, *rest = rest
    acc_refs = rest
    if next_span is not None:
        next_ref, *acc_refs, sems = rest
        start_all(kernel_ref, next_ref, sems, next_span)
    gather_passes(place_ref[0], block_ref, sk_ref, acc_refs, keep_ref, send_ref, chunk, first)
    if next_span is not None:
        wait_all(kernel_ref, next_ref, sems, next_span)


def gathered(place, block, sk_value, kernel, passes, chunk, first, chunk_rows, next_span, partly):
    _, segments, rows, cols = block.shape
    width = sk_value.shape[1]
    piece = pltpu.VMEM((segments // 2, passes, chunk_rows, width // passes), jnp.bfloat16)
    operands = [place, local(block), local(sk_value)]
    in_specs = [in_smem, in_vmem, in_vmem]
    out_shape = [piece, piece]
    scratch = [pltpu.VMEM((2, segments * rows, width // passes), jnp.float32)] * passes
    aliases = {}
    if next_span is not None:
        operands.append(remote(kernel))
        in_specs.append(in_hbm)
        out_shape.append(pltpu.VMEM((2, segments, next_span[1], cols), jnp.bfloat16))
        scratch.append(pltpu.SemaphoreType.DMA((2, segments)))
    if partly is not None:
        aliases = {len(operands): 0, len(operands) + 1: 1}
        operands.extend(map(local, partly))
        in_specs.extend([in_vmem, in_vmem])
    return pl.pallas_call(
        functools.partial(
            gather_body, chunk=chunk, first=first, next_span=next_span, filled=partly is not None
        ),
        name="gather",
        in_specs=in_specs,
        out_specs=[in_vmem] * len(out_shape),
        out_shape=out_shape,
        scratch_shapes=scratch,
        input_output_aliases=aliases,
        compiler_params=params(12),
        cost_estimate=cost_of(kernel, (0, rows), width),
    )(*operands)


def sum_body(*refs, stages):
    for held, got, got_row, hold, send, send_row, own in stages:
        total = refs[held][...].astype(jnp.float32)
        width = total.shape[3]
        if got_row is None:
            total = total + refs[got][...].astype(jnp.float32)
        else:
            rows = total.size // width
            total = total + refs[got][got_row : got_row + rows, :].astype(jnp.float32).reshape(total.shape)
        half = total.shape[0] // 2
        if own is None:
            flat = total[half:].astype(jnp.bfloat16).reshape(-1, width)
            refs[hold][...] = total[:half]
            refs[send][send_row : send_row + flat.shape[0], :] = flat
        else:
            refs[own][...] = total[0].astype(jnp.bfloat16)


def summed(parts, count):
    operands = []
    out_shape = []
    entries = []
    send_row = 0
    for phase, held, got, got_row in parts:
        pieces = 1 << (count - phase)
        passes, chunk_rows, width = held.shape[1:]
        entry = [len(operands), len(operands) + 1, got_row, None, None, None, None]
        operands.extend([local(held), local(got)])
        if phase == count:
            entry[6] = len(out_shape)
            out_shape.append(pltpu.VMEM((passes, chunk_rows, width), jnp.bfloat16))
        else:
            entry[3] = len(out_shape)
            entry[5] = send_row
            send_row += passes * chunk_rows * (pieces // 2)
            out_shape.append(pltpu.VMEM((pieces // 2, passes, chunk_rows, width), jnp.float32))
        entries.append(entry)
    if send_row:
        out_shape.append(pltpu.VMEM((send_row, width), jnp.bfloat16))
    for entry in entries:
        if entry[6] is None:
            entry[3] += len(operands)
            entry[4] = len(operands) + len(out_shape) - 1
        else:
            entry[6] += len(operands)
    results = pl.pallas_call(
        functools.partial(sum_body, stages=tuple(map(tuple, entries))),
        name="sum_parts",
        in_specs=[in_vmem] * len(operands),
        out_specs=[in_vmem] * len(out_shape),
        out_shape=out_shape,
        compiler_params=params(8),
    )(*operands)
    return results


def plan_of(count):
    if count == 2:
        return exchanges
    chunks = len(shares)
    return tuple(
        tuple((step - phase, phase) for phase in range(count) if 0 <= step - phase < chunks)
        for step in range(chunks + count - 1)
    )


def weights_body(proj_ref, inv_ref, *out_refs):
    levels = proj_ref.shape[0]
    rank = proj_ref.shape[4]
    for level in range(levels):
        for half in range(2):
            rows = slice(half * rank, (half + 1) * rank)
            re = inv_ref[level, 0, 0, rows, :]
            im = inv_ref[level, 0, 1, rows, :]
            if level + 1 < levels:
                next_re = proj_ref[level + 1, 0, 0]
                next_im = proj_ref[level + 1, 0, 1]
                re, im = (
                    (product(re, next_re) - product(im, next_im)).astype(jnp.bfloat16),
                    (product(re, next_im) + product(im, next_re)).astype(jnp.bfloat16),
                )
            cols = re.shape[1]
            out_refs[level][half * 2 * rank : half * 2 * rank + rank, :cols] = re
            out_refs[level][half * 2 * rank : half * 2 * rank + rank, cols:] = im
            out_refs[level][half * 2 * rank + rank : (half + 1) * 2 * rank, :cols] = -im
            out_refs[level][half * 2 * rank + rank : (half + 1) * 2 * rank, cols:] = re


def level_weights(projections, inverses):
    levels = projections.shape[0]
    rank = projections.shape[4]
    sketch_cols = inverses.shape[4]
    shapes = [
        pltpu.VMEM((4 * rank, 2 * (rank if level + 1 < levels else sketch_cols)), jnp.bfloat16)
        for level in range(levels)
    ]
    return pl.pallas_call(
        weights_body,
        name="level_weights",
        out_specs=[in_vmem] * levels,
        out_shape=shapes,
        compiler_params=params(8),
    )(projections, inverses)


def paired(own, partner, weight_ref):
    width = own.shape[-1]
    own = own.reshape(-1, width)
    partner = partner.reshape(-1, width)
    return product(own, weight_ref[:width, :]) + product(partner, weight_ref[width:, :])


def middle_body(*refs, count):
    weight_ref = refs[2 * count]
    out_ref = refs[2 * count + 1]
    first = 0
    for place in range(count):
        own = refs[place][...]
        rows = own.shape[1]
        value = paired(own, refs[count + place][...], weight_ref)
        out_ref[:, first : first + rows, :] = value.astype(jnp.bfloat16).reshape(own.shape)
        first += rows


def middle_level(owns, partners, weight):
    passes, _, width = owns[0].shape
    rows = sum(own.shape[1] for own in owns)
    operands = [local(value) for value in (*owns, *partners, weight)]
    return pl.pallas_call(
        functools.partial(middle_body, count=len(owns)),
        name="middle_level",
        in_specs=[in_vmem] * len(operands),
        out_specs=in_vmem,
        out_shape=pltpu.VMEM((passes, rows, width), jnp.bfloat16),
        compiler_params=params(4),
    )(*operands)


def normalized(own_ref, partner_ref, weight_ref, gain_ref):
    current = paired(own_ref[...], partner_ref[...], weight_ref)
    sketch_cols = gain_ref.shape[1]
    power = jnp.sum(current * current, axis=-1, keepdims=True) / sketch_cols
    scale = lax.rsqrt(power + epsilon)
    gain = gain_ref[...]
    shape = own_ref.shape[:2] + (sketch_cols,)
    return (
        (current[:, :sketch_cols] * scale * gain).reshape(shape),
        (current[:, sketch_cols:] * scale * gain).reshape(shape),
    )


def staged_body(own_ref, partner_ref, weight_ref, gain_ref, stage_ref):
    stage_ref[0], stage_ref[1] = normalized(own_ref, partner_ref, weight_ref, gain_ref)


def staged_level(own, partner, weight, gain):
    passes, rows, _ = own.shape
    return pl.pallas_call(
        staged_body,
        name="staged_level",
        in_specs=[in_vmem] * 4,
        out_specs=in_vmem,
        out_shape=pltpu.VMEM((2, passes, rows, gain.shape[1]), jnp.float32),
        compiler_params=params(8),
    )(local(own), local(partner), local(weight), local(gain))


def final_body(own_ref, partner_ref, weight_ref, gain_ref, *rest, firsts):
    stages = rest[: len(firsts) - 1]
    out_ref, stage_ref, sems, pass_sems = rest[len(firsts) - 1 :]
    copies = []
    for place, (first, part_ref) in enumerate(zip(firsts, stages)):
        target = out_ref.at[:, :, pl.ds(first, part_ref.shape[2]), :]
        copies.append(pltpu.make_async_copy(part_ref, target, sems.at[place]))
    for copy in copies:
        copy.start()
    re, im = normalized(own_ref, partner_ref, weight_ref, gain_ref)
    for one in range(stage_ref.shape[1]):
        stage_ref[0, one] = re[one]
        stage_ref[1, one] = im[one]
        target = out_ref.at[:, one, pl.ds(firsts[-1], stage_ref.shape[2]), :]
        copies.append(pltpu.make_async_copy(stage_ref.at[:, one], target, pass_sems.at[one]))
        copies[-1].start()
    for copy in copies:
        copy.wait()


def final_level(own, partner, weight, gain, stages, firsts, segment_rows):
    passes, rows, _ = own.shape
    sketch_cols = gain.shape[1]
    operands = [local(value) for value in (own, partner, weight, gain, *stages)]
    return pl.pallas_call(
        functools.partial(final_body, firsts=tuple(firsts)),
        name="final_level",
        in_specs=[in_vmem] * len(operands),
        out_specs=in_hbm,
        out_shape=jax.ShapeDtypeStruct((2, passes, segment_rows, sketch_cols), jnp.float32),
        scratch_shapes=[
            pltpu.VMEM((2, passes, rows, sketch_cols), jnp.float32),
            pltpu.SemaphoreType.DMA((max(len(firsts) - 1, 1),)),
            pltpu.SemaphoreType.DMA((passes,)),
        ],
        compiler_params=params(8),
    )(*operands)


def shards(kernel, sketch, projections, inverses, norm_gain):
    members = lax.axis_size("sk")
    count = phase_count(members)
    levels = projections.shape[0]
    passes = sketch.shape[0]
    top_bits = lax.axis_size("bf").bit_length() - 1
    _, rows, cols = kernel.shape
    segment_rows = rows // members
    tiles = segment_rows // row_tile
    bounds = [tiles * sum(shares[:end]) // sum(shares) * row_tile for end in range(len(shares) + 1)]
    spans = [(first, last - first) for first, last in zip(bounds, bounds[1:])]
    chunks = len(spans)
    kernel = kernel.reshape(2, members, segment_rows, cols)
    place = lax.axis_index("sk").reshape(1).astype(jnp.int32)
    gain = norm_gain.reshape(1, -1)
    weights = level_weights(projections, inverses)
    keeps = []
    cores = []
    block = None
    pieces = []
    for chunk, span in enumerate(spans):
        rows = span[1] // splits[chunk]
        pieces.extend((chunk, part * rows, (span[0] + part * rows, rows)) for part in range(splits[chunk]))
    filled = None
    for number, (chunk, first, span) in enumerate(pieces):
        next_span = pieces[number + 1][2] if number + 1 < len(pieces) else None
        chunk_rows = spans[chunk][1]
        if number == 0:
            both = [span] if next_span is None else [span, next_span]
            keep, send, sk_value, *blocks = first_gathered(
                place, kernel, sketch, projections, both, chunk_rows
            )
        else:
            keep, send, *blocks = gathered(
                place, block, sk_value, kernel, passes, chunk, first, chunk_rows, next_span, filled
            )
        filled = (keep, send)
        if blocks:
            block = blocks[0]
        if first + span[1] == chunk_rows:
            filled = None
            keeps.append(keep)
            cores.append(swapped(send, "sk", 1))
    held = dict(enumerate(keeps))
    got = {chunk: (core, None) for chunk, core in enumerate(cores)}
    for place, exchange in enumerate(plan_of(count)):
        parts = [(phase, held[chunk], *got[chunk]) for chunk, phase in exchange]
        *kept, send = summed(parts, count)
        chunk, phase = exchange[0]
        received = swapped_step(send, chunk + phase)
        row = 0
        for (chunk, _), value in zip(exchange, kept):
            held[chunk] = value
            got[chunk] = (received, row)
            row += value.size // value.shape[3]
    owns = []
    for chunk in range(chunks):
        owns.extend(summed([(count, held[chunk], *got[chunk])], count))
    partners = []
    for chunk in range(chunks):
        partners.append(swapped(owns[chunk], "bf", 2 ** (top_bits - 1)))
    stages = []
    firsts = []
    for place, group in enumerate(groups):
        own = [owns[chunk] for chunk in group]
        partner = [partners[chunk] for chunk in group]
        for level in range(1, levels):
            merged = middle_level(own, partner, weights[level - 1])
            own = [merged]
            partner = [swapped(merged, "bf", 2 ** (top_bits - 1 - level))]
        firsts.append(spans[group[0]][0])
        if place + 1 < len(groups):
            stages.append(staged_level(own[0], partner[0], weights[levels - 1], gain))
        else:
            out = final_level(
                own[0], partner[0], weights[levels - 1], gain, stages, firsts, segment_rows
            )
    return out


def solution(mesh):
    placed = (
        P(None, "bf", "sk"),
        P(None, "sk", None),
        P(None, "bf", None, None, None),
        P(None, "bf", None, None, None),
        P(),
    )

    return jax.shard_map(
        shards,
        mesh=mesh,
        in_specs=placed,
        out_specs=P(None, None, ("bf", "sk"), None),
        check_vma=False,
    )
```
